128 devices in a mesh: row: 4 (over z), col: 32 (over x, y, core).
Axes of the slice: x: 4, y: 4, z: 4, core: 2. Of those that a mesh axis runs over, the one named last changes fastest.
Arguments:
- star_pos: float32 [512, 3, 128], P(('row', 'col')), may hold values from -5 to 5
- star_vel: float32 [512, 3, 128], P(('row', 'col')), may hold values from -5 to 5
- star_acc: float32 [512, 3, 128], P(('row', 'col')), may hold values from -5 to 5
- star_jerk: float32 [512, 3, 128], P(('row', 'col')), may hold values from -5 to 5
- star_mass: float32 [512, 128], P(('row', 'col')), may hold values from 3.0517578e-05 to 0.00024414062
- active_index: int32 [128, 128], P(('row', 'col')), may hold values from 0 to 511, as said below
- send_block: int32 [128, 128, 4], P(('row', 'col')), may hold values from -1 to 3, as said below
- send_leaf: int32 [128, 128, 4], P(('row', 'col')), may hold values from -1 to 127
- galaxy_pos: float32 [16384, 3, 128], P(('row', 'col')), may hold values from -5 to 5
- galaxy_mass: float32 [16384, 128], P(('row', 'col')), may hold values from 0.0001 to 0.001
Outputs:
- star_pos_new: float32 [512, 3, 128], P(('row', 'col'))
- star_vel_new: float32 [512, 3, 128], P(('row', 'col'))
- galaxy_accel: float32 [16384, 3, 128], P(('row', 'col'))
The draws below stay inside these ranges and needn't reach their ends.
Inputs may be any that keep to these rules, and one draw needn't show every extreme that they name: `active_index`: the entries of one device's row are distinct. `send_block`: an entry is -1 exactly where the same entry of send_leaf is -1. Every device fills all 4 slots to itself, and one device receives 4 filled slots from every device.
All inputs are finite; a program needn't handle non-finite values.
Results may differ from the reference program's by a relative error of at most 0.0003.
Values sent between devices are 32-bit elements; how exact they have to be, the bound alone decides.
No kernel may reach another device: no remote copies, remote signals or barrier semaphores. Data moves between devices by JAX's collectives and lax.ppermute only.
A program may use at most 64 MiB of HBM per device.

```python
import math
import jax
import jax.numpy as jnp
from jax import lax

STAR_DEV = 512
ACT_DEV = 128
LEAF_DEV = 128
SLOTS = 4
BLOCK = 128
LEAF = 128
STARS = 65536
SBLOCKS = 512
LEAVES = 16384
DEVICES = 128


def draw_active_index(key, part):
    keys = jax.random.split(jax.random.fold_in(key, 11), DEVICES)

    def one(item):
        return jax.random.permutation(item, STAR_DEV)[:ACT_DEV]
    return jax.vmap(one)(keys).astype(jnp.int32)


def route_table(key):
    base = jax.random.fold_in(key, 23)
    key_live, key_block, key_leaf, key_hot = jax.random.split(base, 4)
    shape = (DEVICES, DEVICES, SLOTS)
    source = jnp.arange(DEVICES, dtype=jnp.int32)[:, None, None]
    target = jnp.arange(DEVICES, dtype=jnp.int32)[None, :, None]
    hottest = jax.random.randint(key_hot, (), 0, DEVICES)
    live = (jax.random.randint(key_live, shape, 0, 2) == 0) | (target == source) | (target == hottest)
    blocks = jax.random.randint(key_block, shape, 0, STAR_DEV // BLOCK)
    leaves = jax.random.randint(key_leaf, shape, 0, LEAF_DEV)
    return (jnp.where(live, blocks, -1).astype(jnp.int32), jnp.where(live, leaves, -1).astype(jnp.int32))


def draw_send_block(key, part):
    return route_table(key)[0]


def draw_send_leaf(key, part):
    return route_table(key)[1]


def level_of(own_key, shape, cuts, least, largest):
    gain = 1.0
    for position, shards_of in cuts:
        draws = jax.random.uniform(jax.random.fold_in(jax.random.fold_in(own_key, 6), position), (shards_of,), jnp.float32, least / len(cuts), largest / len(cuts))
        gain = gain * jnp.repeat(jnp.exp(draws), shape[position] // shards_of).reshape((-1,) + (1,) * (len(shape) - 1 - position))
    return gain


def normal_values(rng, dims, deviation, bound, cuts=(), held_as=jnp.bfloat16):
    values = deviation * jax.random.normal(rng, dims, jnp.float32)
    if cuts:
        values = values * level_of(rng, dims, cuts, -0.22, 0.18)
    return jnp.clip(values, -bound, bound).astype(held_as)


def setup_inputs(seed: int = 0) -> dict:
    seeds = jax.random.split(jax.random.key(seed), 11)
    star_pos = normal_values(seeds[0], (SBLOCKS, 3, BLOCK), 1.0, 5.0, ((0, 128),), jnp.float32)
    star_vel = normal_values(seeds[1], (SBLOCKS, 3, BLOCK), 1.0, 5.0, ((0, 128),), jnp.float32)
    star_acc = normal_values(seeds[2], (SBLOCKS, 3, BLOCK), 1.0, 5.0, ((0, 128),), jnp.float32)
    star_jerk = normal_values(seeds[3], (SBLOCKS, 3, BLOCK), 1.0, 5.0, ((0, 128),), jnp.float32)
    star_mass = jnp.clip(jnp.exp(math.log(0.00024414062) - 2.0794415 * jax.random.uniform(seeds[4], (SBLOCKS, BLOCK), jnp.float32) ** level_of(seeds[4], (SBLOCKS, BLOCK), ((0, 128),), -0.2, 0.2)), 3.0517578125e-05, 0.00024414062)
    active_index = draw_active_index(jax.random.fold_in(seeds[10], 71), 0)
    send_block = draw_send_block(jax.random.fold_in(seeds[10], 71), 0)
    send_leaf = draw_send_leaf(jax.random.fold_in(seeds[10], 71), 0)
    galaxy_pos = normal_values(seeds[8], (LEAVES, 3, LEAF), 1.0, 5.0, ((0, 128),), jnp.float32)
    galaxy_mass = jnp.clip(jnp.exp(math.log(0.001) - 2.3025852 * jax.random.uniform(seeds[9], (LEAVES, LEAF), jnp.float32) ** level_of(seeds[9], (LEAVES, LEAF), ((0, 128),), -0.2, 0.2)), 0.0001, 0.001)
    return dict(star_pos=star_pos, star_vel=star_vel, star_acc=star_acc, star_jerk=star_jerk, star_mass=star_mass, active_index=active_index, send_block=send_block, send_leaf=send_leaf, galaxy_pos=galaxy_pos, galaxy_mass=galaxy_mass)


step_length = 1.0
soft_star = 0.01
soft_galaxy = 0.04

def pair_block(apos, avel, rpos, rvel, rmass):
    delta = rpos[:, None, :] - apos[:, :, None]
    dvel = rvel[:, None, :] - avel[:, :, None]
    radius = lax.optimization_barrier(jnp.sum(delta * delta, 0)) + soft_star
    inverse = lax.rsqrt(radius)
    weight = rmass[None, :] * inverse * inverse * inverse
    along = lax.optimization_barrier(jnp.sum(delta * dvel, 0)) * inverse * inverse
    accel = lax.optimization_barrier(jnp.sum(delta * weight[None], -1))
    jerks = lax.optimization_barrier(jnp.sum((dvel - 3.0 * along[None] * delta) * weight[None], -1))
    return (accel, jerks)

def entry_terms(stars4, leaves4):
    count = stars4.shape[0]
    group = math.gcd(count, 16)

    def one(item):
        spos = item[0][:, :3]
        smass = item[0][:, 3]
        gpos = item[1][:, :3]
        gmass = item[1][:, 3]
        delta = gpos[:, :, None, :] - spos[:, :, :, None]
        radius = lax.optimization_barrier(jnp.sum(delta * delta, 1)) + soft_galaxy
        inverse = lax.rsqrt(radius)
        cube = inverse * inverse * inverse
        kick = lax.optimization_barrier(jnp.sum(delta * (gmass[:, None, :] * cube)[:, None], -1))
        pull = -lax.optimization_barrier(jnp.sum(delta * (smass[:, :, None] * cube)[:, None], 2))
        return (pull, kick)
    shaped = (stars4.reshape((count // group, group) + stars4.shape[1:]), leaves4.reshape((count // group, group) + leaves4.shape[1:]))
    pull, kick = lax.map(one, shaped)
    return (pull.reshape((count,) + pull.shape[2:]), kick.reshape((count,) + kick.shape[2:]))

def flatten(blocks):
    return blocks.transpose(1, 0, 2).reshape(3, -1)

def reference(star_pos, star_vel, star_acc, star_jerk, star_mass, active_index, send_block, send_leaf, galaxy_pos, galaxy_mass):
    half = 0.5 * step_length ** 2
    sixth = step_length ** 3 / 6.0
    pred_pos = star_pos + step_length * star_vel + half * star_acc + sixth * star_jerk
    pred_vel = star_vel + step_length * star_acc + half * star_jerk
    pos_flat = flatten(pred_pos)
    vel_flat = flatten(pred_vel)
    mass_flat = star_mass.reshape(-1)
    devices = active_index.shape[0]
    chosen = (active_index + jnp.arange(devices, dtype=jnp.int32)[:, None] * STAR_DEV).reshape(-1).astype(jnp.int32)
    apos = pos_flat[:, chosen]
    avel = vel_flat[:, chosen]
    total = apos.shape[1]
    size = math.gcd(total, 512)
    stars = pos_flat.shape[1]
    stretch = math.gcd(stars, 4096)
    rpos = pos_flat.reshape(3, stars // stretch, stretch).transpose(1, 0, 2)
    rvel = vel_flat.reshape(3, stars // stretch, stretch).transpose(1, 0, 2)
    rmass = mass_flat.reshape(stars // stretch, stretch)

    def active_group(item):

        def step(carry, piece):
            accel, jerks = pair_block(item[0], item[1], piece[0], piece[1], piece[2])
            return ((carry[0] + accel, carry[1] + jerks), None)
        start = (jnp.zeros((3, size), jnp.float32), jnp.zeros((3, size), jnp.float32))
        result, unused = lax.scan(step, start, (rpos, rvel, rmass))
        return result
    grouped = (apos.reshape(3, total // size, size).transpose(1, 0, 2), avel.reshape(3, total // size, size).transpose(1, 0, 2))
    acc_new, jerk_new = lax.map(active_group, grouped)
    acc_new = acc_new.transpose(1, 0, 2).reshape(3, total)
    jerk_new = jerk_new.transpose(1, 0, 2).reshape(3, total)
    start_acc = flatten(star_acc)[:, chosen]
    start_jerk = flatten(star_jerk)[:, chosen]
    start_pos = flatten(star_pos)[:, chosen]
    start_vel = flatten(star_vel)[:, chosen]
    vel_one = start_vel + (start_acc + acc_new) * (0.5 * step_length) + (start_jerk - jerk_new) * (step_length ** 2 / 12.0)
    pos_one = start_pos + (start_vel + vel_one) * (0.5 * step_length) + (start_acc - acc_new) * (step_length ** 2 / 12.0)
    nblock = STAR_DEV // BLOCK
    pos_new_flat = pos_flat.at[:, chosen].set(pos_one)
    vel_mid_flat = vel_flat.at[:, chosen].set(vel_one)
    star_pos_new = pos_new_flat.reshape(3, -1, BLOCK).transpose(1, 0, 2)
    vel_mid = vel_mid_flat.reshape(3, -1, BLOCK).transpose(1, 0, 2)
    packed_stars = jnp.concatenate([star_pos_new, star_mass[:, None, :]], 1)
    packed_gal = jnp.concatenate([galaxy_pos, galaxy_mass[:, None, :]], 1)

    def per_source(carry, source):
        table = send_block[source]
        leafs = send_leaf[source]
        live = (table >= 0).reshape(-1).astype(jnp.float32)[:, None, None]
        local_block = jnp.maximum(table, 0).reshape(-1).astype(jnp.int32)
        sidx = (source * nblock + local_block).astype(jnp.int32)
        gidx = (jnp.arange(devices, dtype=jnp.int32)[:, None] * LEAF_DEV + jnp.maximum(leafs, 0)).reshape(-1).astype(jnp.int32)
        stars4 = packed_stars[sidx] * live
        leaves4 = packed_gal[gidx] * live
        pull, kick = entry_terms(stars4, leaves4)
        carry = carry.at[gidx].add(pull)
        kicks = jnp.zeros((nblock, 3, BLOCK), jnp.float32).at[local_block].add(kick)
        return (carry, kicks)
    empty = jnp.zeros(galaxy_pos.shape, jnp.float32)
    pull_total, kicks = lax.scan(per_source, empty, jnp.arange(devices, dtype=jnp.int32))
    kick_all = kicks.reshape(star_pos.shape)
    star_vel_new = vel_mid + step_length * kick_all
    galaxy_accel = pull_total * (STARS / BLOCK)
    return (star_pos_new, star_vel_new, galaxy_accel)
```

```python
import functools

import jax
import jax.numpy as jnp
from jax import lax
from jax.experimental import pallas as pl
from jax.experimental.pallas import tpu as pltpu
from jax.sharding import PartitionSpec as P

F32 = jnp.float32
BF16 = jnp.bfloat16
I32 = jnp.int32

STAR_DEV = 512
BLOCK = 128
STEP = 1.0
SOFT_STAR = 0.01
SOFT_GALAXY = 0.04

NT = (((1,), (1,)), ((), ()))
SMEM = pl.BlockSpec(memory_space=pltpu.SMEM)
VMEM = pl.BlockSpec(memory_space=pltpu.VMEM)


def split3(x):
    a = x.astype(BF16).astype(F32)
    r = x - a
    b = r.astype(BF16).astype(F32)
    c = (r - b).astype(BF16).astype(F32)
    return a, b, c


def predicted(pos, vel, acc, jerk):
    half = 0.5 * STEP**2
    sixth = STEP**3 / 6.0
    return (
        pos + STEP * vel + half * acc + sixth * jerk,
        vel + STEP * acc + half * jerk,
    )


def chosen_hot(active_row, stars):
    row = lax.broadcasted_iota(I32, (stars, active_row.shape[1]), 0)
    return jnp.where(row == active_row, 1.0, 0.0).astype(BF16)


def sum_parts(x):
    n = x.shape[0] // 3
    return x[:n] + x[n : 2 * n] + x[2 * n : 3 * n]


def pre_kernel(pos_ref, vel_ref, acc_ref, jerk_ref, mass_ref, idx_ref, leaf_ref,
               planes_ref, act_ref, start_ref):
    nb = mass_ref.shape[0]
    lanes = lambda ref, q: jnp.concatenate([ref[q, b : b + 1, :] for b in range(nb)], 1)
    rows = lambda ref: jnp.concatenate([lanes(ref, q) for q in range(3)], 0)
    pos, vel, acc, jerk = (rows(r) for r in (pos_ref, vel_ref, acc_ref, jerk_ref))
    mass = jnp.concatenate([mass_ref[b : b + 1, :] for b in range(nb)], 1)
    leaf = jnp.concatenate([leaf_ref[s : s + 1, :] for s in range(leaf_ref.shape[0])], 1)
    x, v = predicted(pos, vel, acc, jerk)
    planes_ref[...] = jnp.concatenate([x, v, mass, leaf.astype(F32)], 0)
    hot = chosen_hot(idx_ref[...], pos.shape[1])
    zero4 = jnp.zeros((4, pos.shape[1]), F32)
    parts = split3(jnp.concatenate([pos, vel, acc, jerk, zero4], 0))
    at = sum_parts(
        jnp.dot(jnp.concatenate(parts, 0).astype(BF16), hot, preferred_element_type=F32)
    )
    start_ref[...] = at
    ax, av = predicted(at[0:3], at[3:6], at[6:9], at[9:12])
    sent = jnp.concatenate([ax, av, jnp.zeros((2, at.shape[1]), F32)], 0)
    for c in range(act_ref.shape[0]):
        act_ref[c] = sent


def prepare(pos, vel, acc, jerk, mass, idx, leaf, cols):
    stars = mass.size
    acts = idx.shape[1]
    return pl.pallas_call(
        pre_kernel,
        out_shape=(
            jax.ShapeDtypeStruct((8, stars), F32),
            jax.ShapeDtypeStruct((cols, 8, acts), F32),
            jax.ShapeDtypeStruct((16, acts), F32),
        ),
    )(pos, vel, acc, jerk, mass, idx, leaf)


def pair_kernel(width, row_ref, act_ref, s0_ref, s1_ref, s2_ref, s3_ref, out_ref,
                rs_ref, b_ref, ws_ref, leaf_ref):
    own = s0_ref.shape[1]
    refs = (s0_ref, s1_ref, s2_ref, s3_ref)
    n = own * len(refs)
    acts = act_ref.shape[2]
    ic = act_ref.shape[0] * acts

    @pl.when(pl.program_id(0) == 0)
    def _():
        for k, ref in enumerate(refs):
            s = ref[...]
            row = lax.broadcasted_iota(I32, s.shape, 0)
            s1, s2, s3 = split3(s)
            x = s[0:3]
            v = s[3:6]
            n1, n2, n3 = split3(jnp.sum(x * x, 0, keepdims=True))
            d1, d2, d3 = split3(jnp.sum(x * v, 0, keepdims=True))
            one = jnp.ones_like(n1)
            zero7 = jnp.zeros((7, own), F32)
            tail = [one, one, one, n1, n2, n3, d1, d2, d3, zero7]
            big = jnp.concatenate([s1, s2, s3, s1, s2, s1] + tail, 0)
            rs_ref[k * own : (k + 1) * own, :] = big.T.astype(BF16)
            m = s[6:7]
            g1, g2, g3 = split3(jnp.where(row == 6, m, s * m))
            b_ref[:, k * own : (k + 1) * own] = jnp.concatenate(
                [g1, g2, g3, jnp.zeros_like(g1)], 0
            ).astype(BF16)
        slots = own // 128
        table = [r[7:8, 128 * s : 128 * s + 128] for r in refs for s in range(slots)]
        table.append(jnp.zeros((128 - len(table), 128), F32))
        turned = pltpu.roll(jnp.concatenate(table, 0), (128 - 32 * row_ref[0]) & 127, 1)
        leaf_ref[...] = turned.T

    a = jnp.concatenate([act_ref[q] for q in range(act_ref.shape[0])], 1)
    x = a[0:3]
    v = a[3:6]
    zero2 = jnp.zeros((2, ic), F32)
    one = jnp.ones((1, ic), F32)
    zero3 = jnp.zeros((3, ic), F32)
    one3 = jnp.ones((3, ic), F32)
    zero7 = jnp.zeros((7, ic), F32)

    def left(p, extra, tail):
        p1, p2, p3 = split3(p)
        return jnp.concatenate(
            [p1, p1, p1, p2, p2, p3] + list(split3(extra)) + tail + [zero7], 0
        )

    lr = left(
        jnp.concatenate([-2.0 * x, zero3, zero2], 0),
        jnp.sum(x * x, 0, keepdims=True) + SOFT_STAR,
        [one3, zero3],
    )
    lv = left(
        jnp.concatenate([-v, -x, zero2], 0),
        jnp.sum(x * v, 0, keepdims=True),
        [zero3, one3],
    )
    L = jnp.concatenate([lr, lv], 1).astype(BF16)
    f = None
    for j0 in range(0, n, width):
        p = jnp.dot(rs_ref[j0 : j0 + width, :], L, preferred_element_type=F32)
        inv = lax.rsqrt(p[:, :ic])
        i2 = inv * inv
        w = i2 * inv
        ws_ref[j0 : j0 + width, :ic] = w.astype(BF16)
        ws_ref[j0 : j0 + width, ic:] = ((w * i2) * p[:, ic:]).astype(BF16)
        d = jnp.dot(
            b_ref[:, j0 : j0 + width],
            ws_ref[j0 : j0 + width, :],
            preferred_element_type=F32,
        )
        f = d if f is None else f + d
    t = sum_parts(f[0:24])
    wt = t[:, :ic]
    st = t[:, ic:]
    mw = wt[6:7]
    ms = st[6:7]
    acc = wt[0:3] - x * mw
    jerk = wt[3:6] - v * mw - 3.0 * (st[0:3] - x * ms)
    for q in range(act_ref.shape[0]):
        cut = slice(q * acts, (q + 1) * acts)
        c = pl.program_id(0) * act_ref.shape[0] + q
        out_ref[q, 0:6, :] = jnp.concatenate([acc[:, cut], jerk[:, cut]], 0)
        out_ref[q, 6:7, :] = leaf_ref[pl.ds(c, 1), :]
        out_ref[q, 7:8, :] = jnp.zeros((1, acts), F32)


def pair_terms(row, active, stars, group=2, width=1024):
    cols, _, acts = active.shape
    own = stars[0].shape[1]
    n = own * len(stars)
    ic = group * acts
    block = pl.BlockSpec((group, 8, acts), lambda i: (i, 0, 0))
    whole = pl.BlockSpec((8, own), lambda i: (0, 0))
    return pl.pallas_call(
        functools.partial(pair_kernel, width),
        grid=(cols // group,),
        in_specs=[SMEM, block] + [whole] * len(stars),
        out_specs=block,
        out_shape=jax.ShapeDtypeStruct((cols, 8, acts), F32),
        scratch_shapes=[
            pltpu.VMEM((n, 64), BF16),
            pltpu.VMEM((32, n), BF16),
            pltpu.VMEM((n, 2 * ic), BF16),
            pltpu.VMEM((128, 128), F32),
        ],
    )(row, active, *stars)


def correct_kernel(block_ref, part_ref, start_ref, planes_ref, idx_ref,
                   pos_ref, mid_ref, send_ref, table_ref, lo_ref, hi_ref):
    nb = pos_ref.shape[1]
    total = part_ref[0]
    for c in range(1, part_ref.shape[0]):
        total = total + part_ref[c]
    table_ref[...] = part_ref[:, 6, :].astype(I32)
    acc = total[0:3]
    jerk = total[3:6]
    x0, v0, a0, j0 = (start_ref[3 * q : 3 * q + 3, :] for q in range(4))
    v1 = v0 + (a0 + acc) * (0.5 * STEP) + (j0 - jerk) * (STEP**2 / 12.0)
    x1 = x0 + (v0 + v1) * (0.5 * STEP) + (a0 - acc) * (STEP**2 / 12.0)
    one = jnp.ones((2, x1.shape[1]), F32)
    parts = split3(jnp.concatenate([x1, v1, one], 0))
    planes = planes_ref[...]
    hot = chosen_hot(idx_ref[...], planes.shape[1])
    put = jnp.concatenate(parts + (jnp.zeros_like(parts[0]),), 0).astype(BF16)
    spread = sum_parts(lax.dot_general(put, hot, NT, preferred_element_type=F32)[0:24])
    new = jnp.where(spread[6:7] > 0.5, spread, planes)
    zero4 = jnp.zeros((4, BLOCK), F32)
    for b in range(nb):
        cut = slice(b * BLOCK, (b + 1) * BLOCK)
        for q in range(3):
            pos_ref[q, b : b + 1, :] = new[q : q + 1, cut]
            mid_ref[q, b : b + 1, :] = new[3 + q : 4 + q, cut]
        packed = jnp.concatenate([new[0:3, cut], planes[6:7, cut]], 0)
        lo_ref[b] = jnp.concatenate([packed, zero4], 0)
        hi_ref[b] = jnp.concatenate([zero4, packed], 0)
    lo_ref[nb] = jnp.concatenate([zero4, zero4], 0)
    hi_ref[nb] = jnp.concatenate([zero4, zero4], 0)

    def body(e, carry):
        for h in range(2):
            a = block_ref[2 * h, e]
            b = block_ref[2 * h + 1, e]
            send_ref[e, 8 * h : 8 * h + 8, :] = (
                lo_ref[jnp.where(a < 0, nb, a)] + hi_ref[jnp.where(b < 0, nb, b)]
            )
        return carry

    lax.fori_loop(0, send_ref.shape[0], body, 0, unroll=8)


def correct(block, part, start, planes, idx, nb):
    targets = block.shape[1]
    return pl.pallas_call(
        correct_kernel,
        in_specs=[SMEM] + [VMEM] * 4,
        out_shape=(
            jax.ShapeDtypeStruct((3, nb, BLOCK), F32),
            jax.ShapeDtypeStruct((3, nb, BLOCK), F32),
            jax.ShapeDtypeStruct((targets, 16, BLOCK), F32),
            jax.ShapeDtypeStruct((part.shape[0], 128), I32),
        ),
        scratch_shapes=[pltpu.VMEM((nb + 1, 8, BLOCK), F32)] * 2,
    )(block, part, start, planes, idx)


def leaf_kernel(pos_ref, mass_ref, g_ref, gm_ref):
    def body(l, carry):
        g = jnp.concatenate([pos_ref[q, pl.ds(l, 1), :] for q in range(3)], 0)
        m = mass_ref[pl.ds(l, 1), :]
        z1 = jnp.zeros_like(m)
        z4 = jnp.zeros((4, m.shape[1]), F32)
        e = jnp.concatenate(split3(jnp.sum(g * g, 0, keepdims=True) + SOFT_GALAXY), 0)
        p1, p2, p3 = split3(-2.0 * g)
        low = []
        high = []
        for t in (p1, p1, p1, p2, p2, p3, jnp.ones_like(g), e):
            low += [t, z1, z4]
            high += [z4, t, z1]
        g_ref[l] = jnp.concatenate(low + high, 0).T.astype(BF16)
        w1, w2, w3 = split3(jnp.concatenate([g * m, m], 0))
        gm_ref[l] = jnp.concatenate([w1, w1, w2, w2, w3, w3, z4, z4], 0).astype(BF16)
        return carry

    lax.fori_loop(0, mass_ref.shape[0], body, 0, unroll=4)


def leaf_prep(pos, mass):
    nl = mass.shape[0]
    return pl.pallas_call(
        leaf_kernel,
        out_shape=(
            jax.ShapeDtypeStruct((nl, 128, 128), BF16),
            jax.ShapeDtypeStruct((nl, 32, 128), BF16),
        ),
        cost_estimate=pl.CostEstimate(
            flops=10**7, transcendentals=0, bytes_accessed=5 * 10**6
        ),
    )(pos, mass)


def entry_kernel(G, scale, row_ref, tab_ref, st_ref, g_ref, gm_ref, gpos_ref,
                 pull_ref, kick_ref, acc_ref, t_ref, s_ref, v_ref):
    nl = g_ref.shape[0]
    ng = 2 * st_ref.shape[0] // G
    acc_ref[...] = jnp.zeros_like(acc_ref)
    t_ref[...] = jnp.zeros_like(t_ref)
    r8 = lax.broadcasted_iota(I32, (8, 128), 0)
    low = r8 < 4
    q4 = r8 & 3
    one = jnp.ones((8, 128), F32)
    zero8 = jnp.zeros((8, 128), F32)
    me = row_ref[0]

    def leaves(g, j):
        d = g * (G // 2) + j // 2
        h = j % 2
        c = d & 31
        k = (me - lax.shift_right_logical(d, 5)) & 3
        la = jnp.maximum(tab_ref[c, k * 4 + 2 * h], 0)
        lb = jnp.maximum(tab_ref[c, k * 4 + 2 * h + 1], 0)
        return la, lb

    def halves(t, a, b):
        return jnp.where(
            low,
            jnp.broadcast_to(t[a : a + 1], (8, 128)),
            jnp.broadcast_to(t[b : b + 1], (8, 128)),
        )

    def stars(g, j):
        h = 8 * (j % 2)
        return st_ref[g * (G // 2) + j // 2, h : h + 8, :]

    def prep(g, b, j):
        s = stars(g, j)
        s1, s2, s3 = split3(s)
        x2 = jnp.where(q4 == 3, 0.0, s * s)
        x2 = x2 + jnp.where((r8 & 1) == 0, pltpu.roll(x2, 7, 0), pltpu.roll(x2, 1, 0))
        x2 = x2 + jnp.where((r8 & 2) == 0, pltpu.roll(x2, 6, 0), pltpu.roll(x2, 2, 0))
        n1, n2, n3 = split3(x2)
        t1 = jnp.where(q4 == 0, n1, jnp.where(q4 == 1, n2, n3))
        T = jnp.concatenate([s1, s2, s3, s1, s2, s1, t1, one], 0).astype(BF16)
        t_ref[b, j, 0:64, 0:128] = T
        t_ref[b, j, 64:128, 128:256] = T
        m1, m2, m3 = split3(jnp.where(q4 == 3, s, s * halves(s, 3, 7)))
        s_ref[b, j] = jnp.concatenate([m1, m2, m3, zero8], 0).astype(BF16)

    def force(g, b, j):
        la, lb = leaves(g, j)
        lane = lax.broadcasted_iota(I32, (128, 128), 1)
        L = jnp.where(lane < 64, g_ref[la], g_ref[lb])
        inv = lax.rsqrt(jnp.dot(L, t_ref[b, j], preferred_element_type=F32))
        u = inv * inv * inv
        hi = u.astype(BF16)
        v_ref[b, j, 0:128, :] = hi
        v_ref[b, j, 128:256, :] = (u - hi.astype(F32)).astype(BF16)

    def sums(g, b, j):
        la, lb = leaves(g, j)
        h = 8 * (j % 2)
        r32 = lax.broadcasted_iota(I32, (32, 128), 0)
        gm = jnp.where((r32 & 7) < 4, gm_ref[la], gm_ref[lb])
        f = jnp.dot(jnp.concatenate([gm, gm], 1), v_ref[b, j], preferred_element_type=F32)
        t = sum_parts(f[0:24])
        t = jnp.where(low, t[:, :128], t[:, 128:])
        kick_ref[g * (G // 2) + j // 2, h : h + 8, :] = t - stars(g, j) * halves(t, 3, 7)
        S = s_ref[b, j]
        hi = v_ref[b, j, 0:128, :]
        lo = v_ref[b, j, 128:256, :]
        V = jnp.concatenate(
            [
                jnp.concatenate([hi[:, :128], lo[:, :128]], 1),
                jnp.concatenate([hi[:, 128:], lo[:, 128:]], 1),
            ],
            0,
        )
        f = lax.dot_general(jnp.concatenate([S, S], 1), V, NT, preferred_element_type=F32)
        return la, lb, sum_parts(f[0:24])

    def step(g, b, more, more2):
        done = []
        for j in range(G):
            done.append(sums(g, b, j))
            if more:
                force(g + 1, 1 - b, j)
            if more2:
                prep(g + 2, b, j)
        for la, lb, t in done:
            acc_ref[la] += jnp.where(low, t[:, :128], 0.0)
            acc_ref[lb] += jnp.where(low, 0.0, t[:, 128:])

    for j in range(G):
        prep(0, 0, j)
    for j in range(G):
        force(0, 0, j)
        prep(1, 1, j)

    def body(i, carry):
        step(2 * i, 0, True, True)
        step(2 * i + 1, 1, True, True)
        return carry

    lax.fori_loop(0, ng // 2 - 1, body, 0)
    step(ng - 2, 0, True, False)
    step(ng - 1, 1, False, False)

    def finish(l, carry):
        a = acc_ref[l]
        a = a[0:4] + a[4:8]
        for q in range(3):
            g = gpos_ref[q, pl.ds(l, 1), :]
            pull_ref[q, pl.ds(l, 1), :] = (a[q : q + 1] - g * a[3:4]) * scale
        return carry

    lax.fori_loop(0, nl, finish, 0, unroll=8)


def entry_terms(row, table, stars, g, gm, gpos, scale, G=4):
    nd = stars.shape[0]
    nl = g.shape[0]
    return pl.pallas_call(
        functools.partial(entry_kernel, G, scale),
        in_specs=[SMEM] * 2 + [VMEM] * 4,
        out_shape=(
            jax.ShapeDtypeStruct((3, nl, 128), F32),
            jax.ShapeDtypeStruct((nd, 16, 128), F32),
        ),
        scratch_shapes=[
            pltpu.VMEM((nl, 8, 128), F32),
            pltpu.VMEM((2, G, 128, 256), BF16),
            pltpu.VMEM((2, G, 32, 128), BF16),
            pltpu.VMEM((2, G, 256, 256), BF16),
        ],
    )(row, table, stars, g, gm, gpos)


def finish_kernel(block_ref, kick_ref, mid_ref, vel_ref):
    nb = mid_ref.shape[1]
    low = lax.broadcasted_iota(I32, (8, 128), 0) < 4

    def body(e, sums):
        sums = list(sums)
        for h in range(2):
            owner = jnp.where(low, block_ref[2 * h, e], block_ref[2 * h + 1, e])
            k = kick_ref[e, 8 * h : 8 * h + 8, :]
            for b in range(nb):
                sums[b] = sums[b] + jnp.where(owner == b, k, 0.0)
        return tuple(sums)

    start = tuple(jnp.zeros((8, 128), F32) for _ in range(nb))
    sums = lax.fori_loop(0, kick_ref.shape[0], body, start, unroll=8)
    for b in range(nb):
        total = sums[b][0:4] + sums[b][4:8]
        for q in range(3):
            vel_ref[q, b : b + 1, :] = mid_ref[q, b : b + 1, :] + STEP * total[q : q + 1]


def finish(block, kicks, mid):
    return pl.pallas_call(
        finish_kernel,
        in_specs=[SMEM] + [VMEM] * 2,
        out_shape=jax.ShapeDtypeStruct(mid.shape, F32),
    )(block, kicks, mid)


def local(
    star_pos,
    star_vel,
    star_acc,
    star_jerk,
    star_mass,
    active_index,
    send_block,
    send_leaf,
    galaxy_pos,
    galaxy_mass,
):
    rows = lax.axis_size("row")
    cols = lax.axis_size("col")
    nb = star_pos.shape[0]
    turn = lambda x: x.transpose(1, 0, 2)
    row = lax.axis_index("row").astype(I32).reshape(1)
    block = send_block[0].T
    leaf = send_leaf[0].T
    gpos = turn(galaxy_pos)
    planes, sent, start = prepare(
        turn(star_pos), turn(star_vel), turn(star_acc), turn(star_jerk),
        star_mass, active_index, leaf, cols,
    )
    stars = [planes]
    for k in range(1, rows):
        perm = [(i, (i + k) % rows) for i in range(rows)]
        stars.append(lax.ppermute(planes, "row", perm))
    active = lax.all_to_all(sent, "col", 0, 0, tiled=True)
    parts = pair_terms(row, active, stars)
    parts = lax.all_to_all(parts, "col", 0, 0, tiled=True)
    pos_new, mid, outgoing, table = correct(block, parts, start, planes, active_index, nb)
    arrived = lax.all_to_all(outgoing, ("row", "col"), 0, 0, tiled=True)
    g, gm = leaf_prep(gpos, galaxy_mass)
    scale = STAR_DEV * rows * cols / BLOCK
    pull, kick = entry_terms(row, table, arrived, g, gm, gpos, scale)
    returned = lax.all_to_all(kick, ("row", "col"), 0, 0, tiled=True)
    vel_new = finish(block, returned, mid)
    return turn(pos_new), turn(vel_new), turn(pull)


def solution(mesh):
    both = P(("row", "col"), None, None)
    flat = P(("row", "col"), None)
    return jax.shard_map(
        local,
        mesh=mesh,
        in_specs=(both, both, both, both, flat, flat, both, both, both, flat),
        out_specs=(both, both, both),
        check_vma=False,
    )
```

```python
import functools

import jax
import jax.numpy as jnp
from jax import lax
from jax.experimental import pallas as pl
from jax.experimental.pallas import tpu as pltpu
from jax.sharding import PartitionSpec as P


F32 = jnp.float32
BF16 = jnp.bfloat16
I32 = jnp.int32

STAR_DEV = 512
BLOCK = 128
STEP = 1.0
SOFT_STAR = 0.01
SOFT_GALAXY = 0.04

NT = (((1,), (1,)), ((), ()))
SMEM = pl.BlockSpec(memory_space=pltpu.SMEM)
VMEM = pl.BlockSpec(memory_space=pltpu.VMEM)


def grant(mib):
    return pltpu.CompilerParams(vmem_limit_bytes=mib * 2**20)


def split3(x):
    a = x.astype(BF16).astype(F32)
    r = x - a
    b = r.astype(BF16).astype(F32)
    c = (r - b).astype(BF16).astype(F32)
    return a, b, c


def predicted(pos, vel, acc, jerk):
    half = 0.5 * STEP**2
    sixth = STEP**3 / 6.0
    return (
        pos + STEP * vel + half * acc + sixth * jerk,
        vel + STEP * acc + half * jerk,
    )


def chosen_hot(active_row, stars):
    row = lax.broadcasted_iota(I32, (stars, active_row.shape[1]), 0)
    return jnp.where(row == active_row, 1.0, 0.0).astype(BF16)


def sum_parts(x):
    n = x.shape[0] // 3
    return x[:n] + x[n : 2 * n] + x[2 * n : 3 * n]


def pre_kernel(pos_ref, vel_ref, acc_ref, jerk_ref, mass_ref, idx_ref, leaf_ref, block_ref,
               planes_ref, act_ref, start_ref, hot_ref):
    nb = mass_ref.shape[0]
    lanes = lambda ref, q: jnp.concatenate([ref[q, b : b + 1, :] for b in range(nb)], 1)
    rows = lambda ref: jnp.concatenate([lanes(ref, q) for q in range(3)], 0)
    flat = lambda ref: jnp.concatenate([ref[b : b + 1, :] for b in range(ref.shape[0])], 1)
    pos, vel, acc, jerk = (rows(r) for r in (pos_ref, vel_ref, acc_ref, jerk_ref))
    x, v = predicted(pos, vel, acc, jerk)
    zero1 = jnp.zeros((1, pos.shape[1]), F32)
    planes_ref[0:8, :] = jnp.concatenate([x, v, flat(mass_ref), zero1], 0)
    lists = [flat(leaf_ref).astype(F32), flat(block_ref).astype(F32)]
    planes_ref[8:16, :] = jnp.concatenate(lists + [zero1] * 6, 0)
    hot = chosen_hot(idx_ref[...], pos.shape[1])
    hot_ref[...] = hot
    zero4 = jnp.zeros((4, pos.shape[1]), F32)
    parts = split3(jnp.concatenate([pos, vel, acc, jerk, zero4], 0))
    at = sum_parts(
        jnp.dot(jnp.concatenate(parts, 0).astype(BF16), hot, preferred_element_type=F32)
    )
    start_ref[...] = at
    ax, av = predicted(at[0:3], at[3:6], at[6:9], at[9:12])
    act_ref[...] = jnp.concatenate([ax, av, jnp.zeros((2, at.shape[1]), F32)], 0)


def prepare(pos, vel, acc, jerk, mass, idx, leaf, block):
    stars = mass.size
    acts = idx.shape[1]
    return pl.pallas_call(
        pre_kernel,
        out_shape=(
            jax.ShapeDtypeStruct((16, stars), F32),
            jax.ShapeDtypeStruct((8, acts), F32),
            jax.ShapeDtypeStruct((16, acts), F32),
            jax.ShapeDtypeStruct((stars, acts), BF16),
        ),
    )(pos, vel, acc, jerk, mass, idx, leaf, block)


def address_kernel(cols, row_ref, act_ref, s0_ref, s1_ref, s2_ref, s3_ref, out_ref):
    refs = (s0_ref, s1_ref, s2_ref, s3_ref)
    slots = s0_ref.shape[1] // 128
    table = [
        ref[q : q + 1, 128 * s : 128 * s + 128]
        for q in range(2)
        for ref in refs
        for s in range(slots)
    ]
    table.append(jnp.zeros((128 - len(table), 128), F32))
    shift = (128 - cols * row_ref[0]) & 127
    turned = pltpu.roll(jnp.concatenate(table, 0), shift, 1).T
    for c in range(cols):
        out_ref[c, 0:6, :] = act_ref[0:6, :]
        out_ref[c, 6:7, :] = turned[c : c + 1, :]
        out_ref[c, 7:8, :] = jnp.zeros((1, 128), F32)


def address(row, active, stars, cols):
    lists = pl.BlockSpec((8, stars[0].shape[1]), lambda i: (1, 0))
    whole = pl.BlockSpec(active.shape, lambda i: (0, 0))
    return pl.pallas_call(
        functools.partial(address_kernel, cols),
        grid=(1,),
        in_specs=[SMEM, whole] + [lists] * len(stars),
        out_specs=pl.BlockSpec((cols,) + active.shape, lambda i: (0, 0, 0)),
        out_shape=jax.ShapeDtypeStruct((cols,) + active.shape, F32),
        compiler_params=grant(8),
    )(row, active, *stars)


def pair_kernel(width, act_ref, s0_ref, s1_ref, s2_ref, s3_ref, out_ref,
                rs_ref, b_ref, ws_ref):
    own = s0_ref.shape[1]
    refs = (s0_ref, s1_ref, s2_ref, s3_ref)
    n = own * len(refs)
    acts = act_ref.shape[2]
    ic = act_ref.shape[0] * acts

    @pl.when(pl.program_id(0) == 0)
    def _():
        for k, ref in enumerate(refs):
            s = ref[...]
            row = lax.broadcasted_iota(I32, s.shape, 0)
            s1, s2, s3 = split3(s)
            x = s[0:3]
            v = s[3:6]
            n1, n2, n3 = split3(jnp.sum(x * x, 0, keepdims=True))
            d1, d2, d3 = split3(jnp.sum(x * v, 0, keepdims=True))
            one = jnp.ones_like(n1)
            zero7 = jnp.zeros((7, own), F32)
            tail = [one, one, one, n1, n2, n3, d1, d2, d3, zero7]
            big = jnp.concatenate([s1, s2, s3, s1, s2, s1] + tail, 0)
            rs_ref[k * own : (k + 1) * own, :] = big.T.astype(BF16)
            m = s[6:7]
            g1, g2, g3 = split3(jnp.where(row == 6, m, s * m))
            b_ref[:, k * own : (k + 1) * own] = jnp.concatenate(
                [g1, g2, g3, jnp.zeros_like(g1)], 0
            ).astype(BF16)

    a = jnp.concatenate([act_ref[q] for q in range(act_ref.shape[0])], 1)
    x = a[0:3]
    v = a[3:6]
    zero2 = jnp.zeros((2, ic), F32)
    one = jnp.ones((1, ic), F32)
    zero3 = jnp.zeros((3, ic), F32)
    one3 = jnp.ones((3, ic), F32)
    zero7 = jnp.zeros((7, ic), F32)

    def left(p, extra, tail):
        p1, p2, p3 = split3(p)
        return jnp.concatenate(
            [p1, p1, p1, p2, p2, p3] + list(split3(extra)) + tail + [zero7], 0
        )

    lr = left(
        jnp.concatenate([-2.0 * x, zero3, zero2], 0),
        jnp.sum(x * x, 0, keepdims=True) + SOFT_STAR,
        [one3, zero3],
    )
    lv = left(
        jnp.concatenate([-v, -x, zero2], 0),
        jnp.sum(x * v, 0, keepdims=True),
        [zero3, one3],
    )
    L = jnp.concatenate([lr, lv], 1).astype(BF16)
    f = None
    for j0 in range(0, n, width):
        p = jnp.dot(rs_ref[j0 : j0 + width, :], L, preferred_element_type=F32)
        inv = lax.rsqrt(p[:, :ic])
        i2 = inv * inv
        w = i2 * inv
        ws_ref[j0 : j0 + width, :ic] = w.astype(BF16)
        ws_ref[j0 : j0 + width, ic:] = ((w * i2) * p[:, ic:]).astype(BF16)
        d = jnp.dot(
            b_ref[:, j0 : j0 + width],
            ws_ref[j0 : j0 + width, :],
            preferred_element_type=F32,
        )
        f = d if f is None else f + d
    t = sum_parts(f[0:24])
    wt = t[:, :ic]
    st = t[:, ic:]
    mw = wt[6:7]
    ms = st[6:7]
    acc = wt[0:3] - x * mw
    jerk = wt[3:6] - v * mw - 3.0 * (st[0:3] - x * ms)
    for q in range(act_ref.shape[0]):
        cut = slice(q * acts, (q + 1) * acts)
        out_ref[q] = jnp.concatenate([acc[:, cut], jerk[:, cut], zero2[:, cut]], 0)


def pair_terms(active, stars, group=2, width=1024):
    cols, _, acts = active.shape
    own = stars[0].shape[1]
    n = own * len(stars)
    ic = group * acts
    block = pl.BlockSpec((group, 8, acts), lambda i: (i, 0, 0))
    whole = pl.BlockSpec((8, own), lambda i: (0, 0))
    return pl.pallas_call(
        functools.partial(pair_kernel, width),
        grid=(cols // group,),
        in_specs=[block] + [whole] * len(stars),
        out_specs=block,
        out_shape=jax.ShapeDtypeStruct((cols, 8, acts), F32),
        compiler_params=grant(16),
        scratch_shapes=[
            pltpu.VMEM((n, 64), BF16),
            pltpu.VMEM((32, n), BF16),
            pltpu.VMEM((n, 2 * ic), BF16),
        ],
        cost_estimate=pl.CostEstimate(
            flops=4 * 2 * 128 * cols * acts * n,
            transcendentals=cols * acts * n,
            bytes_accessed=4 * 2 * cols * 8 * acts,
        ),
    )(active, *stars)


def correct_kernel(part_ref, start_ref, planes_ref, hot_ref, pos_ref, mid_ref, send_ref):
    nb = pos_ref.shape[1]
    total = part_ref[0]
    for c in range(1, part_ref.shape[0]):
        total = total + part_ref[c]
    acc = total[0:3]
    jerk = total[3:6]
    x0, v0, a0, j0 = (start_ref[3 * q : 3 * q + 3, :] for q in range(4))
    v1 = v0 + (a0 + acc) * (0.5 * STEP) + (j0 - jerk) * (STEP**2 / 12.0)
    x1 = x0 + (v0 + v1) * (0.5 * STEP) + (a0 - acc) * (STEP**2 / 12.0)
    one = jnp.ones((2, x1.shape[1]), F32)
    parts = split3(jnp.concatenate([x1, v1, one], 0))
    planes = planes_ref[0:8, :]
    put = jnp.concatenate(parts + (jnp.zeros_like(parts[0]),), 0).astype(BF16)
    spread = sum_parts(
        lax.dot_general(put, hot_ref[...], NT, preferred_element_type=F32)[0:24]
    )
    new = jnp.where(spread[6:7] > 0.5, spread, planes)
    sent = []
    for b in range(nb):
        cut = slice(b * BLOCK, (b + 1) * BLOCK)
        for q in range(3):
            pos_ref[q, b : b + 1, :] = new[q : q + 1, cut]
            mid_ref[q, b : b + 1, :] = new[3 + q : 4 + q, cut]
        sent += [new[0:3, cut], planes[6:7, cut]]
    sent = jnp.concatenate(sent, 0)
    for e in range(send_ref.shape[0]):
        send_ref[e] = sent


def correct(part, start, planes, hot, nb, chips):
    return pl.pallas_call(
        correct_kernel,
        in_specs=[VMEM] * 4,
        out_shape=(
            jax.ShapeDtypeStruct((3, nb, BLOCK), F32),
            jax.ShapeDtypeStruct((3, nb, BLOCK), F32),
            jax.ShapeDtypeStruct((chips, 4 * nb, BLOCK), F32),
        ),
    )(part, start, planes, hot)


def target_terms(g):
    z1 = jnp.zeros((1, g.shape[1]), F32)
    z4 = jnp.zeros((4, g.shape[1]), F32)
    e = jnp.concatenate(split3(jnp.sum(g * g, 0, keepdims=True) + SOFT_GALAXY), 0)
    p1, p2, p3 = split3(-2.0 * g)
    low = []
    high = []
    for t in (p1, p1, p1, p2, p2, p3, jnp.ones_like(g), e):
        low += [t, z1, z4]
        high += [z4, t, z1]
    return jnp.concatenate(low + high, 0).T.astype(BF16)


def leaf_kernel(pos_ref, mass_ref, g_ref, lo_ref, hi_ref):
    nl = mass_ref.shape[0]
    z4 = jnp.zeros((4, 128), F32)

    def body(l, carry):
        g = jnp.concatenate([pos_ref[q, pl.ds(l, 1), :] for q in range(3)], 0)
        m = mass_ref[pl.ds(l, 1), :]
        g_ref[l] = target_terms(g)
        lo_ref[l] = jnp.concatenate([g, m, z4], 0)
        hi_ref[l] = jnp.concatenate([z4, g, m], 0)
        return carry

    lax.fori_loop(0, nl, body, 0, unroll=4)
    lo_ref[nl] = jnp.zeros((8, 128), F32)
    hi_ref[nl] = jnp.zeros((8, 128), F32)


def leaf_prep(pos, mass):
    nl = mass.shape[0]
    return pl.pallas_call(
        leaf_kernel,
        out_shape=(
            jax.ShapeDtypeStruct((nl, 128, 128), BF16),
            jax.ShapeDtypeStruct((nl + 1, 8, 128), F32),
            jax.ShapeDtypeStruct((nl + 1, 8, 128), F32),
        ),
        cost_estimate=pl.CostEstimate(
            flops=10**7, transcendentals=0, bytes_accessed=7 * 10**6
        ),
    )(pos, mass)


def listed(row, d):
    return d & 31, 4 * ((row - lax.shift_right_logical(d, 5)) & 3)


def fetch_kernel(row_ref, tab_ref, lo_ref, hi_ref, out_ref):
    nl = lo_ref.shape[0] - 1
    row = row_ref[0]

    def body(d, carry):
        c, k = listed(row, d)
        for h in range(2):
            a = tab_ref[c, k + 2 * h]
            b = tab_ref[c, k + 2 * h + 1]
            out_ref[d, 8 * h : 8 * h + 8, :] = (
                lo_ref[jnp.where(a < 0, nl, a)] + hi_ref[jnp.where(b < 0, nl, b)]
            )
        return carry

    lax.fori_loop(0, out_ref.shape[0], body, 0, unroll=8)


def fetch(row, table, lo, hi, sources):
    return pl.pallas_call(
        fetch_kernel,
        in_specs=[SMEM] * 2 + [VMEM] * 2,
        out_shape=jax.ShapeDtypeStruct((sources, 16, 128), F32),
    )(row, table, lo, hi)


def attract(G, ng, bodies, targets, g_ref, acc_ref, t_ref, s_ref, v_ref):
    acc_ref[...] = jnp.zeros_like(acc_ref)
    t_ref[...] = jnp.zeros_like(t_ref)
    r8 = lax.broadcasted_iota(I32, (8, 128), 0)
    low = r8 < 4
    q4 = r8 & 3
    one = jnp.ones((8, 128), F32)
    zero8 = jnp.zeros((8, 128), F32)

    def prep(g, b, j):
        s = bodies(g, j, low)
        s1, s2, s3 = split3(s)
        x2 = jnp.where(q4 == 3, 0.0, s * s)
        x2 = x2 + jnp.where((r8 & 1) == 0, pltpu.roll(x2, 7, 0), pltpu.roll(x2, 1, 0))
        x2 = x2 + jnp.where((r8 & 2) == 0, pltpu.roll(x2, 6, 0), pltpu.roll(x2, 2, 0))
        n1, n2, n3 = split3(x2)
        t1 = jnp.where(q4 == 0, n1, jnp.where(q4 == 1, n2, n3))
        T = jnp.concatenate([s1, s2, s3, s1, s2, s1, t1, one], 0).astype(BF16)
        t_ref[b, j, 0:64, 0:128] = T
        t_ref[b, j, 64:128, 128:256] = T
        m = jnp.where(
            low,
            jnp.broadcast_to(s[3:4], (8, 128)),
            jnp.broadcast_to(s[7:8], (8, 128)),
        )
        m1, m2, m3 = split3(jnp.where(q4 == 3, s, s * m))
        s_ref[b, j] = jnp.concatenate([m1, m2, m3, zero8], 0).astype(BF16)

    def force(g, b, j):
        la, lb = targets(g, j)
        lane = lax.broadcasted_iota(I32, (128, 128), 1)
        L = jnp.where(lane < 64, g_ref[la], g_ref[lb])
        inv = lax.rsqrt(jnp.dot(L, t_ref[b, j], preferred_element_type=F32))
        u = inv * inv * inv
        hi = u.astype(BF16)
        lo = (u - hi.astype(F32)).astype(BF16)
        v_ref[b, j, 0:128, 0:128] = hi[:, :128]
        v_ref[b, j, 0:128, 128:256] = lo[:, :128]
        v_ref[b, j, 128:256, 0:128] = hi[:, 128:]
        v_ref[b, j, 128:256, 128:256] = lo[:, 128:]

    def sums(g, b, j):
        S = s_ref[b, j]
        f = lax.dot_general(
            jnp.concatenate([S, S], 1), v_ref[b, j], NT, preferred_element_type=F32
        )
        return targets(g, j) + (sum_parts(f[0:24]),)

    def step(g, b, more, more2):
        done = []
        for j in range(G):
            done.append(sums(g, b, j))
            if more:
                force(g + 1, 1 - b, j)
            if more2:
                prep(g + 2, b, j)
        for la, lb, t in done:
            acc_ref[la] += jnp.where(low, t[:, :128], 0.0)
            acc_ref[lb] += jnp.where(low, 0.0, t[:, 128:])

    for j in range(G):
        prep(0, 0, j)
    for j in range(G):
        force(0, 0, j)
        prep(1, 1, j)

    def body(i, carry):
        step(2 * i, 0, True, True)
        step(2 * i + 1, 1, True, True)
        return carry

    lax.fori_loop(0, ng // 2 - 1, body, 0)
    step(ng - 2, 0, True, False)
    step(ng - 1, 1, False, False)


def attract_scratch(targets, G):
    return [
        pltpu.VMEM((targets, 8, 128), F32),
        pltpu.VMEM((2, G, 128, 256), BF16),
        pltpu.VMEM((2, G, 32, 128), BF16),
        pltpu.VMEM((2, G, 256, 256), BF16),
    ]


def attract_cost(entries):
    return pl.CostEstimate(
        flops=3 * 2 * entries * 128**3,
        transcendentals=entries * 128**2,
        bytes_accessed=entries * 4 * 512,
    )


def kick_kernel(G, block_ref, leaf_ref, pos_ref, mid_ref, vel_ref, g_ref, *scratch):
    nb = pos_ref.shape[1]
    acc_ref = scratch[0]
    place = [
        jnp.concatenate([pos_ref[q, b : b + 1, :] for q in range(3)], 0) for b in range(nb)
    ]
    for b in range(nb):
        g_ref[b] = target_terms(place[b])

    def where(g, j):
        e = g * (G // 2) + j // 2
        h = 2 * (j % 2)
        return jnp.maximum(block_ref[h, e], 0), jnp.maximum(block_ref[h + 1, e], 0)

    def bodies(g, j, low):
        h = 8 * (j % 2)
        return leaf_ref[g * (G // 2) + j // 2, h : h + 8, :]

    attract(G, 2 * leaf_ref.shape[0] // G, bodies, where, g_ref, *scratch)
    for b in range(nb):
        a = acc_ref[b]
        a = a[0:4] + a[4:8]
        kick = a[0:3] - place[b] * a[3:4]
        for q in range(3):
            vel_ref[q, b : b + 1, :] = mid_ref[q, b : b + 1, :] + STEP * kick[q : q + 1]


def kicks(block, leaves, pos, mid, G=4):
    nb = pos.shape[1]
    return pl.pallas_call(
        functools.partial(kick_kernel, G),
        in_specs=[SMEM] + [VMEM] * 3,
        out_shape=jax.ShapeDtypeStruct(mid.shape, F32),
        scratch_shapes=[pltpu.VMEM((nb, 128, 128), BF16)] + attract_scratch(nb, G),
        cost_estimate=attract_cost(4 * leaves.shape[0]),
    )(block, leaves, pos, mid)


def pull_kernel(G, scale, here_ref, tab_ref, own_ref, other_ref, g_ref, gpos_ref,
                pull_ref, *scratch):
    acc_ref = scratch[0]
    row = here_ref[0]
    core = here_ref[1]

    def source(g, j):
        i = g * (G // 4) + j // 4
        flip = (j // 2) % 2
        c, k = listed(row, 2 * i + (core ^ flip))
        return (own_ref, other_ref)[flip], i, c, k + 2 * (j % 2)

    def where(g, j):
        _, _, c, k = source(g, j)
        return jnp.maximum(tab_ref[c, k], 0), jnp.maximum(tab_ref[c, k + 1], 0)

    def bodies(g, j, low):
        ref, i, c, k = source(g, j)
        a = tab_ref[c, 16 + k]
        b = tab_ref[c, 16 + k + 1]
        ta = ref[i, lax.shift_right_logical(jnp.maximum(a, 0), 1)]
        tb = ref[i, lax.shift_right_logical(jnp.maximum(b, 0), 1)]
        ta = jnp.where((a & 1) == 1, pltpu.roll(ta, 4, 0), ta)
        tb = jnp.where((b & 1) == 1, tb, pltpu.roll(tb, 4, 0))
        return jnp.where(jnp.where(low, a, b) < 0, 0.0, jnp.where(low, ta, tb))

    ng = 4 * own_ref.shape[0] // G
    attract(G, ng, bodies, where, g_ref, *scratch)

    def finish(l, carry):
        a = acc_ref[l]
        a = a[0:4] + a[4:8]
        for q in range(3):
            g = gpos_ref[q, pl.ds(l, 1), :]
            pull_ref[q, pl.ds(l, 1), :] = (a[q : q + 1] - g * a[3:4]) * scale
        return carry

    lax.fori_loop(0, g_ref.shape[0], finish, 0, unroll=8)


def pulls(here, table, own, other, g, gpos, scale, G=4):
    nl = g.shape[0]
    return pl.pallas_call(
        functools.partial(pull_kernel, G, scale),
        in_specs=[SMEM] * 2 + [VMEM] * 4,
        out_shape=jax.ShapeDtypeStruct((3, nl, 128), F32),
        scratch_shapes=attract_scratch(nl, G),
        cost_estimate=attract_cost(8 * own.shape[0]),
    )(here, table, own, other, g, gpos)


def local(
    star_pos,
    star_vel,
    star_acc,
    star_jerk,
    star_mass,
    active_index,
    send_block,
    send_leaf,
    galaxy_pos,
    galaxy_mass,
):
    rows = lax.axis_size("row")
    cols = lax.axis_size("col")
    devices = rows * cols
    nb = star_pos.shape[0]
    both = ("row", "col")
    turn = lambda x: x.transpose(1, 0, 2)
    row = lax.axis_index("row").astype(I32).reshape(1)
    core = (lax.axis_index("col") & 1).astype(I32).reshape(1)
    here = jnp.concatenate([row, core])
    block = send_block[0].T
    gpos = turn(galaxy_pos)
    planes, active, start, hot = prepare(
        turn(star_pos), turn(star_vel), turn(star_acc), turn(star_jerk),
        star_mass, active_index, send_leaf[0].T, block,
    )
    stars = [planes]
    for k in range(1, rows):
        perm = [(i, (i + k) % rows) for i in range(rows)]
        stars.append(lax.ppermute(planes, "row", perm))
    sent = address(here, active, stars, cols)
    arrived = lax.all_to_all(sent, "col", 0, 0, tiled=True)
    table = arrived[:, 6, :].astype(I32)
    g, lo, hi = leaf_prep(gpos, galaxy_mass)
    leaves = fetch(here, table, lo, hi, devices)
    leaves = lax.all_to_all(leaves, both, 0, 0, tiled=True)
    parts = pair_terms(arrived, stars)
    parts = lax.all_to_all(parts, "col", 0, 0, tiled=True)
    pos_new, mid, outgoing = correct(parts, start, planes, hot, nb, devices // 2)
    same_core = [[d for d in range(devices) if d % 2 == c] for c in range(2)]
    own = lax.all_to_all(outgoing, both, 0, 0, tiled=True, axis_index_groups=same_core)
    other = lax.ppermute(own, "col", [(i, i ^ 1) for i in range(cols)])
    vel_new = kicks(block, leaves, pos_new, mid)
    tiles = lambda x: x.reshape(-1, 2, 8, BLOCK)
    scale = STAR_DEV * devices / BLOCK
    pull = pulls(here, table, tiles(own), tiles(other), g, gpos, scale)
    return turn(pos_new), turn(vel_new), turn(pull)


def solution(mesh):
    both = P(("row", "col"), None, None)
    flat = P(("row", "col"), None)
    return jax.shard_map(
        local,
        mesh=mesh,
        in_specs=(both, both, both, both, flat, flat, both, both, both, flat),
        out_specs=(both, both, both),
        check_vma=False,
    )
```

```python
import functools

import jax
import jax.numpy as jnp
from jax import lax
from jax.experimental import pallas as pl
from jax.experimental.pallas import tpu as pltpu
from jax.sharding import PartitionSpec as P


F32 = jnp.float32
BF16 = jnp.bfloat16
I32 = jnp.int32

STAR_DEV = 512
BLOCK = 128
STEP = 1.0
SOFT_STAR = 0.01
SOFT_GALAXY = 0.04

NT = (((1,), (1,)), ((), ()))
SMEM = pl.BlockSpec(memory_space=pltpu.SMEM)
VMEM = pl.BlockSpec(memory_space=pltpu.VMEM)
HBM = pl.BlockSpec(memory_space=pltpu.HBM)


def grant(mib):
    return pltpu.CompilerParams(vmem_limit_bytes=mib * 2**20)


def split3(x):
    a = x.astype(BF16).astype(F32)
    r = x - a
    b = r.astype(BF16).astype(F32)
    c = (r - b).astype(BF16).astype(F32)
    return a, b, c


def predicted(pos, vel, acc, jerk):
    half = 0.5 * STEP**2
    sixth = STEP**3 / 6.0
    return (
        pos + STEP * vel + half * acc + sixth * jerk,
        vel + STEP * acc + half * jerk,
    )


def chosen_hot(active_row, stars):
    row = lax.broadcasted_iota(I32, (stars, active_row.shape[1]), 0)
    return jnp.where(row == active_row, 1.0, 0.0).astype(BF16)


def sum_parts(x):
    n = x.shape[0] // 3
    return x[:n] + x[n : 2 * n] + x[2 * n : 3 * n]


def pre_kernel(pos_ref, vel_ref, acc_ref, jerk_ref, mass_ref, idx_ref, leaf_ref, block_ref,
               planes_ref, start_ref, hot_ref):
    nb = mass_ref.shape[0]
    lanes = lambda ref, q: jnp.concatenate([ref[q, b : b + 1, :] for b in range(nb)], 1)
    rows = lambda ref: jnp.concatenate([lanes(ref, q) for q in range(3)], 0)
    flat = lambda ref: jnp.concatenate([ref[b : b + 1, :] for b in range(ref.shape[0])], 1)
    pos, vel, acc, jerk = (rows(r) for r in (pos_ref, vel_ref, acc_ref, jerk_ref))
    x, v = predicted(pos, vel, acc, jerk)
    zero1 = jnp.zeros((1, pos.shape[1]), F32)
    planes_ref[0:8, :] = jnp.concatenate([x, v, flat(mass_ref), zero1], 0)
    lists = [flat(leaf_ref).astype(F32), flat(block_ref).astype(F32)]
    planes_ref[8:10, :] = jnp.concatenate(lists, 0)
    hot = chosen_hot(idx_ref[...], pos.shape[1])
    hot_ref[...] = hot
    zero4 = jnp.zeros((4, pos.shape[1]), F32)
    parts = split3(jnp.concatenate([pos, vel, acc, jerk, zero4], 0))
    at = sum_parts(
        jnp.dot(jnp.concatenate(parts, 0).astype(BF16), hot, preferred_element_type=F32)
    )
    start_ref[...] = at
    ax, av = predicted(at[0:3], at[3:6], at[6:9], at[9:12])
    rest = jnp.zeros((6, pos.shape[1] - at.shape[1]), F32)
    planes_ref[10:16, :] = jnp.concatenate([jnp.concatenate([ax, av], 0), rest], 1)


def prepare(pos, vel, acc, jerk, mass, idx, leaf, block):
    stars = mass.size
    acts = idx.shape[1]
    return pl.pallas_call(
        pre_kernel,
        out_shape=(
            jax.ShapeDtypeStruct((16, stars), F32),
            jax.ShapeDtypeStruct((16, acts), F32),
            jax.ShapeDtypeStruct((stars, acts), BF16),
        ),
    )(pos, vel, acc, jerk, mass, idx, leaf, block)


def address_kernel(row_ref, s0_ref, s1_ref, s2_ref, s3_ref, out_ref):
    cols = out_ref.shape[0]
    refs = (s0_ref, s1_ref, s2_ref, s3_ref)
    slots = s0_ref.shape[1] // 128
    table = [
        ref[8 + q : 9 + q, 128 * s : 128 * s + 128]
        for q in range(2)
        for ref in refs
        for s in range(slots)
    ]
    table.append(jnp.zeros((128 - len(table), 128), F32))
    shift = (128 - cols * row_ref[0]) & 127
    turned = pltpu.roll(jnp.concatenate(table, 0), shift, 1).T
    active = s0_ref[10:16, 0:128]
    for c in range(cols):
        out_ref[c, 0:6, :] = active
        out_ref[c, 6:7, :] = turned[c : c + 1, :]
        out_ref[c, 7:8, :] = jnp.zeros((1, 128), F32)


def address(row, stars, cols):
    return pl.pallas_call(
        address_kernel,
        in_specs=[SMEM] + [VMEM] * len(stars),
        out_shape=jax.ShapeDtypeStruct((cols, 8, 128), F32),
        compiler_params=grant(8),
    )(row, *stars)


def pair_kernel(width, act_ref, s0_ref, s1_ref, s2_ref, s3_ref, out_ref,
                rs_ref, b_ref, ws_ref):
    own = s0_ref.shape[1]
    refs = (s0_ref, s1_ref, s2_ref, s3_ref)
    n = own * len(refs)
    acts = act_ref.shape[2]
    ic = act_ref.shape[0] * acts

    @pl.when(pl.program_id(0) == 0)
    def _():
        for k, ref in enumerate(refs):
            s = ref[...]
            row = lax.broadcasted_iota(I32, s.shape, 0)
            s1, s2, s3 = split3(s)
            x = s[0:3]
            v = s[3:6]
            n1, n2, n3 = split3(jnp.sum(x * x, 0, keepdims=True))
            d1, d2, d3 = split3(jnp.sum(x * v, 0, keepdims=True))
            one = jnp.ones_like(n1)
            zero7 = jnp.zeros((7, own), F32)
            tail = [one, one, one, n1, n2, n3, d1, d2, d3, zero7]
            big = jnp.concatenate([s1, s2, s3, s1, s2, s1] + tail, 0)
            rs_ref[k * own : (k + 1) * own, :] = big.T.astype(BF16)
            m = s[6:7]
            g1, g2, g3 = split3(jnp.where(row == 6, m, s * m))
            b_ref[:, k * own : (k + 1) * own] = jnp.concatenate(
                [g1, g2, g3, jnp.zeros_like(g1)], 0
            ).astype(BF16)

    a = jnp.concatenate([act_ref[q] for q in range(act_ref.shape[0])], 1)
    x = a[0:3]
    v = a[3:6]
    zero2 = jnp.zeros((2, ic), F32)
    one = jnp.ones((1, ic), F32)
    zero3 = jnp.zeros((3, ic), F32)
    one3 = jnp.ones((3, ic), F32)
    zero7 = jnp.zeros((7, ic), F32)

    def left(p, extra, tail):
        p1, p2, p3 = split3(p)
        return jnp.concatenate(
            [p1, p1, p1, p2, p2, p3] + list(split3(extra)) + tail + [zero7], 0
        )

    lr = left(
        jnp.concatenate([-2.0 * x, zero3, zero2], 0),
        jnp.sum(x * x, 0, keepdims=True) + SOFT_STAR,
        [one3, zero3],
    )
    lv = left(
        jnp.concatenate([-v, -x, zero2], 0),
        jnp.sum(x * v, 0, keepdims=True),
        [zero3, one3],
    )
    L = jnp.concatenate([lr, lv], 1).astype(BF16)
    f = None
    for j0 in range(0, n, width):
        p = jnp.dot(rs_ref[j0 : j0 + width, :], L, preferred_element_type=F32)
        inv = lax.rsqrt(p[:, :ic])
        i2 = inv * inv
        w = i2 * inv
        ws_ref[j0 : j0 + width, :ic] = w.astype(BF16)
        ws_ref[j0 : j0 + width, ic:] = ((w * i2) * p[:, ic:]).astype(BF16)
        d = jnp.dot(
            b_ref[:, j0 : j0 + width],
            ws_ref[j0 : j0 + width, :],
            preferred_element_type=F32,
        )
        f = d if f is None else f + d
    t = sum_parts(f[0:24])
    wt = t[:, :ic]
    st = t[:, ic:]
    mw = wt[6:7]
    ms = st[6:7]
    acc = wt[0:3] - x * mw
    jerk = wt[3:6] - v * mw - 3.0 * (st[0:3] - x * ms)
    for q in range(act_ref.shape[0]):
        cut = slice(q * acts, (q + 1) * acts)
        out_ref[q] = jnp.concatenate([acc[:, cut], jerk[:, cut], zero2[:, cut]], 0)


def pair_terms(active, stars, group=2, width=1024):
    cols, _, acts = active.shape
    own = stars[0].shape[1]
    n = own * len(stars)
    ic = group * acts
    block = pl.BlockSpec((group, 8, acts), lambda i: (i, 0, 0))
    whole = pl.BlockSpec((8, own), lambda i: (0, 0))
    return pl.pallas_call(
        functools.partial(pair_kernel, width),
        grid=(cols // group,),
        in_specs=[block] + [whole] * len(stars),
        out_specs=block,
        out_shape=jax.ShapeDtypeStruct((cols, 8, acts), F32),
        compiler_params=grant(16),
        scratch_shapes=[
            pltpu.VMEM((n, 64), BF16),
            pltpu.VMEM((32, n), BF16),
            pltpu.VMEM((n, 2 * ic), BF16),
        ],
        cost_estimate=pl.CostEstimate(
            flops=4 * 2 * 128 * cols * acts * n,
            transcendentals=cols * acts * n,
            bytes_accessed=4 * 2 * cols * 8 * acts,
        ),
    )(active, *stars)


def correct_kernel(part_ref, start_ref, planes_ref, hot_ref, pos_ref, mid_ref, send_ref):
    nb = pos_ref.shape[1]
    total = part_ref[0]
    for c in range(1, part_ref.shape[0]):
        total = total + part_ref[c]
    acc = total[0:3]
    jerk = total[3:6]
    x0, v0, a0, j0 = (start_ref[3 * q : 3 * q + 3, :] for q in range(4))
    v1 = v0 + (a0 + acc) * (0.5 * STEP) + (j0 - jerk) * (STEP**2 / 12.0)
    x1 = x0 + (v0 + v1) * (0.5 * STEP) + (a0 - acc) * (STEP**2 / 12.0)
    one = jnp.ones((2, x1.shape[1]), F32)
    parts = split3(jnp.concatenate([x1, v1, one], 0))
    planes = planes_ref[0:8, :]
    put = jnp.concatenate(parts + (jnp.zeros_like(parts[0]),), 0).astype(BF16)
    spread = sum_parts(
        lax.dot_general(put, hot_ref[...], NT, preferred_element_type=F32)[0:24]
    )
    new = jnp.where(spread[6:7] > 0.5, spread, planes)
    sent = []
    for b in range(nb):
        cut = slice(b * BLOCK, (b + 1) * BLOCK)
        for q in range(3):
            pos_ref[q, b : b + 1, :] = new[q : q + 1, cut]
            mid_ref[q, b : b + 1, :] = new[3 + q : 4 + q, cut]
        sent += [new[0:3, cut], planes[6:7, cut]]
    sent = jnp.concatenate(sent, 0)
    for e in range(send_ref.shape[0]):
        send_ref[e] = sent


def correct(part, start, planes, hot, nb, chips):
    return pl.pallas_call(
        correct_kernel,
        in_specs=[VMEM] * 4,
        out_shape=(
            jax.ShapeDtypeStruct((3, nb, BLOCK), F32),
            jax.ShapeDtypeStruct((3, nb, BLOCK), F32),
            jax.ShapeDtypeStruct((chips, 4 * nb, BLOCK), F32),
        ),
    )(part, start, planes, hot)


def target_terms(g):
    z1 = jnp.zeros((1, g.shape[1]), F32)
    z4 = jnp.zeros((4, g.shape[1]), F32)
    e = jnp.concatenate(split3(jnp.sum(g * g, 0, keepdims=True) + SOFT_GALAXY), 0)
    p1, p2, p3 = split3(-2.0 * g)
    low = []
    high = []
    for t in (p1, p1, p1, p2, p2, p3, jnp.ones_like(g), e):
        low += [t, z1, z4]
        high += [z4, t, z1]
    return jnp.concatenate(low + high, 0).T.astype(BF16)


def leaf_kernel(first, pos_ref, mass_ref, g_ref, lo_ref):
    z4 = jnp.zeros((4, 128), F32)

    def body(i, carry):
        l = first + i
        g = jnp.concatenate([pos_ref[q, pl.ds(l, 1), :] for q in range(3)], 0)
        g_ref[i] = target_terms(g)
        lo_ref[i] = jnp.concatenate([g, mass_ref[pl.ds(l, 1), :], z4], 0)
        return carry

    lax.fori_loop(0, g_ref.shape[0], body, 0, unroll=4)


def leaf_prep(pos, mass, part, parts):
    nl = mass.shape[0] // parts
    return pl.pallas_call(
        functools.partial(leaf_kernel, part * nl),
        out_shape=(
            jax.ShapeDtypeStruct((nl, 128, 128), BF16),
            jax.ShapeDtypeStruct((nl, 8, 128), F32),
        ),
        cost_estimate=pl.CostEstimate(
            flops=10**7, transcendentals=0, bytes_accessed=3 * 10**6
        ),
    )(pos, mass)


def gathered(parts, into, sems):
    n = parts[0].shape[0]
    return [
        pltpu.make_async_copy(p, into.at[i * n : (i + 1) * n], sems.at[i])
        for i, p in enumerate(parts)
    ]


def fetch_kernel(rows, row_ref, tab_ref, *refs):
    parts = refs[:-3]
    out_ref, lo_ref, sems = refs[-3:]
    nl = lo_ref.shape[0] - 1
    copies = gathered(parts, lo_ref, sems)
    for copy in copies:
        copy.start()
    lo_ref[nl] = jnp.zeros((8, 128), F32)
    for copy in copies:
        copy.wait()
    cols = out_ref.shape[0] // rows
    for r in range(rows):
        k = 4 * ((row_ref[0] - r) & 3)

        def body(c, carry):
            for h in range(2):
                a = lo_ref[tab_ref[c, k + 2 * h]]
                b = lo_ref[tab_ref[c, k + 2 * h + 1]]
                out_ref[r * cols + c, 8 * h : 8 * h + 8, :] = a + pltpu.roll(b, 4, 0)
            return carry

        lax.fori_loop(0, cols, body, 0, unroll=8)


def fetch(row, table, parts, rows, sources):
    nl = sum(p.shape[0] for p in parts)
    return pl.pallas_call(
        functools.partial(fetch_kernel, rows),
        in_specs=[SMEM] * 2 + [HBM] * len(parts),
        out_shape=jax.ShapeDtypeStruct((sources, 16, 128), F32),
        scratch_shapes=[
            pltpu.VMEM((nl + 1, 8, 128), F32),
            pltpu.SemaphoreType.DMA((len(parts),)),
        ],
    )(row, table, *parts)


def attract(G, ng, fine, bodies, targets, ready, g_ref, acc_ref, t_ref, s_ref, v_ref):
    acc_ref[...] = jnp.zeros_like(acc_ref)
    r8 = lax.broadcasted_iota(I32, (8, 128), 0)
    low = r8 < 4
    q4 = r8 & 3
    one = jnp.ones((8, 128), F32)
    zero8 = jnp.zeros((8, 128), F32)
    zero64 = jnp.zeros((64, 128), BF16)

    def prep(g, b, j):
        s = bodies(g, j, low)
        s1, s2, s3 = split3(s)
        x2 = jnp.where(q4 == 3, 0.0, s * s)
        x2 = x2 + jnp.where((r8 & 1) == 0, pltpu.roll(x2, 7, 0), pltpu.roll(x2, 1, 0))
        x2 = x2 + jnp.where((r8 & 2) == 0, pltpu.roll(x2, 6, 0), pltpu.roll(x2, 2, 0))
        n1, n2, n3 = split3(x2)
        t1 = jnp.where(q4 == 0, n1, jnp.where(q4 == 1, n2, n3))
        m = jnp.where(
            low,
            jnp.broadcast_to(s[3:4], (8, 128)),
            jnp.broadcast_to(s[7:8], (8, 128)),
        )
        for q, t in enumerate((s1, s2, s3, t1)):
            t_ref[b, j, 8 * q : 8 * q + 8, :] = t
        for q, t in enumerate(split3(jnp.where(q4 == 3, s, s * m))):
            s_ref[b, j, 8 * q : 8 * q + 8, :] = t

    def force(g, b, j):
        la, lb = targets(g, j)
        lane = lax.broadcasted_iota(I32, (128, 128), 1)
        L = jnp.where(lane < 64, g_ref[la], g_ref[lb])
        s1, s2, s3, t1 = (t_ref[b, j, 8 * q : 8 * q + 8, :] for q in range(4))
        T = jnp.concatenate([s1, s2, s3, s1, s2, s1, t1, one], 0).astype(BF16)
        W = jnp.concatenate(
            [jnp.concatenate([T, zero64], 1), jnp.concatenate([zero64, T], 1)], 0
        )
        inv = lax.rsqrt(jnp.dot(L, W, preferred_element_type=F32))
        v_ref[b, j] = inv * inv * inv

    def sums(g, b, j):
        S = jnp.concatenate([s_ref[b, j], zero8], 0).astype(BF16)
        u = v_ref[b, j]
        hi = u.astype(BF16)
        if fine:
            lo = (u - hi.astype(F32)).astype(BF16)
            S = jnp.concatenate([S, S], 1)
            V = [jnp.concatenate([t[:, :128] for t in (hi, lo)], 1)]
            V.append(jnp.concatenate([t[:, 128:] for t in (hi, lo)], 1))
        else:
            V = [hi[:, :128], hi[:, 128:]]
        f = lax.dot_general(S, jnp.concatenate(V, 0), NT, preferred_element_type=F32)
        return targets(g, j) + (sum_parts(f[0:24]),)

    def step(g, b, more, more2):
        done = []
        for j in range(G):
            done.append(sums(g, b, j))
            if more:
                force(g + 1, 1 - b, j)
            if more2:
                prep(g + 2, b, j)
        for la, lb, t in done:
            acc_ref[la] += jnp.where(low, t[:, :128], 0.0)
            acc_ref[lb] += jnp.where(low, 0.0, t[:, 128:])

    for j in range(G):
        prep(0, 0, j)
        prep(1, 1, j)
    ready()
    for j in range(G):
        force(0, 0, j)

    def body(i, carry):
        step(2 * i, 0, True, True)
        step(2 * i + 1, 1, True, True)
        return carry

    lax.fori_loop(0, ng // 2 - 1, body, 0)
    step(ng - 2, 0, True, False)
    step(ng - 1, 1, False, False)


def attract_scratch(targets, G):
    return [
        pltpu.VMEM((targets, 8, 128), F32),
        pltpu.VMEM((2, G, 32, 128), F32),
        pltpu.VMEM((2, G, 24, 128), F32),
        pltpu.VMEM((2, G, 128, 256), F32),
    ]


def attract_cost(entries):
    return pl.CostEstimate(
        flops=3 * 2 * entries * 128**3,
        transcendentals=entries * 128**2,
        bytes_accessed=entries * 4 * 512,
    )


def kick_kernel(G, block_ref, leaf_ref, pos_ref, mid_ref, vel_ref, g_ref, *scratch):
    nb = pos_ref.shape[1]
    acc_ref = scratch[0]
    place = [
        jnp.concatenate([pos_ref[q, b : b + 1, :] for q in range(3)], 0) for b in range(nb)
    ]
    for b in range(nb):
        g_ref[b] = target_terms(place[b])

    def where(g, j):
        e = g * (G // 2) + j // 2
        h = 2 * (j % 2)
        return jnp.maximum(block_ref[h, e], 0), jnp.maximum(block_ref[h + 1, e], 0)

    def bodies(g, j, low):
        h = 8 * (j % 2)
        return leaf_ref[g * (G // 2) + j // 2, h : h + 8, :]

    attract(G, 2 * leaf_ref.shape[0] // G, False, bodies, where, lambda: None, g_ref, *scratch)
    for b in range(nb):
        a = acc_ref[b]
        a = a[0:4] + a[4:8]
        kick = a[0:3] - place[b] * a[3:4]
        for q in range(3):
            vel_ref[q, b : b + 1, :] = mid_ref[q, b : b + 1, :] + STEP * kick[q : q + 1]


def kicks(block, leaves, pos, mid, G=16):
    nb = pos.shape[1]
    return pl.pallas_call(
        functools.partial(kick_kernel, G),
        in_specs=[SMEM] + [VMEM] * 3,
        out_shape=jax.ShapeDtypeStruct(mid.shape, F32),
        scratch_shapes=[pltpu.VMEM((nb, 128, 128), BF16)] + attract_scratch(nb, G),
        cost_estimate=attract_cost(4 * leaves.shape[0]),
    )(block, leaves, pos, mid)


def pull_kernel(G, scale, nparts, here_ref, tab_ref, own_ref, other_ref, *refs):
    parts = refs[:nparts]
    far_ref, pull_ref, g_ref, gpos_ref, sems = refs[nparts : nparts + 5]
    scratch = refs[nparts + 5 :]
    acc_ref = scratch[0]
    row = here_ref[0]
    core = here_ref[1]
    copies = gathered(parts, g_ref, sems)
    copies.append(pltpu.make_async_copy(far_ref, gpos_ref, sems.at[nparts]))
    for copy in copies:
        copy.start()

    def ready():
        for copy in copies:
            copy.wait()

    def listed(row, d):
        return d & 31, 4 * ((row - lax.shift_right_logical(d, 5)) & 3)

    def source(g, j):
        i = g * (G // 4) + j // 4
        flip = (j // 2) % 2
        c, k = listed(row, 2 * i + (core ^ flip))
        return (own_ref, other_ref)[flip], i, c, k + 2 * (j % 2)

    def where(g, j):
        _, _, c, k = source(g, j)
        last = g_ref.shape[0] - 1
        return jnp.minimum(tab_ref[c, k], last), jnp.minimum(tab_ref[c, k + 1], last)

    def bodies(g, j, low):
        ref, i, c, k = source(g, j)
        a = tab_ref[c, 16 + k]
        b = tab_ref[c, 16 + k + 1]
        ta = ref[i, lax.shift_right_logical(a, 1) & 1]
        tb = ref[i, lax.shift_right_logical(b, 1) & 1]
        ta = jnp.where((a & 1) == 1, pltpu.roll(ta, 4, 0), ta)
        tb = jnp.where((b & 1) == 1, tb, pltpu.roll(tb, 4, 0))
        return jnp.where(jnp.where(low, a, b) > 3, 0.0, jnp.where(low, ta, tb))

    ng = 4 * own_ref.shape[0] // G
    attract(G, ng, True, bodies, where, ready, g_ref, *scratch)

    def finish(l, carry):
        a = acc_ref[l]
        a = a[0:4] + a[4:8]
        for q in range(3):
            g = gpos_ref[q, pl.ds(l, 1), :]
            pull_ref[q, pl.ds(l, 1), :] = (a[q : q + 1] - g * a[3:4]) * scale
        return carry

    lax.fori_loop(0, g_ref.shape[0], finish, 0, unroll=8)


def pulls(here, table, own, other, parts, gpos, scale, G=16):
    nl = gpos.shape[1]
    return pl.pallas_call(
        functools.partial(pull_kernel, G, scale, len(parts)),
        in_specs=[SMEM] * 2 + [VMEM] * 2 + [HBM] * (len(parts) + 1),
        out_shape=jax.ShapeDtypeStruct((3, nl, 128), F32),
        compiler_params=grant(51),
        scratch_shapes=[
            pltpu.VMEM((nl, 128, 128), BF16),
            pltpu.VMEM(gpos.shape, F32),
            pltpu.SemaphoreType.DMA((len(parts) + 1,)),
        ]
        + attract_scratch(nl, G),
        cost_estimate=attract_cost(8 * own.shape[0]),
    )(here, table, own, other, *parts, gpos)


def local(
    star_pos,
    star_vel,
    star_acc,
    star_jerk,
    star_mass,
    active_index,
    send_block,
    send_leaf,
    galaxy_pos,
    galaxy_mass,
):
    rows = lax.axis_size("row")
    cols = lax.axis_size("col")
    devices = rows * cols
    nb = star_pos.shape[0]
    both = ("row", "col")
    turn = lambda x: x.transpose(1, 0, 2)
    row = lax.axis_index("row").astype(I32).reshape(1)
    core = (lax.axis_index("col") & 1).astype(I32).reshape(1)
    here = jnp.concatenate([row, core])
    block = send_block[0].T
    gpos = turn(galaxy_pos)
    planes, start, hot = prepare(
        turn(star_pos), turn(star_vel), turn(star_acc), turn(star_jerk),
        star_mass, active_index, send_leaf[0].T, block,
    )
    stars = [planes]
    for k in range(1, rows):
        perm = [(i, (i + k) % rows) for i in range(rows)]
        stars.append(lax.ppermute(planes, "row", perm))
    sent = address(here, stars, cols)
    arrived = lax.all_to_all(sent, "col", 0, 0, tiled=True)
    table = arrived[:, 6, :].astype(I32)
    table = jnp.where(table < 0, galaxy_pos.shape[0], table)
    halves = []
    for q in range(2):
        halves.append(leaf_prep(gpos, galaxy_mass, q, 2))
    leaves = fetch(here, table, [t[1] for t in halves], rows, devices)
    leaves = lax.all_to_all(leaves, both, 0, 0, tiled=True)
    parts = pair_terms(arrived, stars)
    parts = lax.all_to_all(parts, "col", 0, 0, tiled=True)
    pos_new, mid, outgoing = correct(parts, start, planes, hot, nb, devices // 2)
    same_core = [[d for d in range(devices) if d % 2 == c] for c in range(2)]
    own = lax.all_to_all(outgoing, both, 0, 0, tiled=True, axis_index_groups=same_core)
    other = lax.ppermute(own, "col", [(i, i ^ 1) for i in range(cols)])
    vel_new = kicks(block, leaves, pos_new, mid)
    tiles = lambda x: x.reshape(-1, 2, 8, BLOCK)
    scale = STAR_DEV * devices / BLOCK
    pull = pulls(
        here, table, tiles(own), tiles(other), [t[0] for t in halves], gpos, scale
    )
    return turn(pos_new), turn(vel_new), turn(pull)


def solution(mesh):
    both = P(("row", "col"), None, None)
    flat = P(("row", "col"), None)
    return jax.shard_map(
        local,
        mesh=mesh,
        in_specs=(both, both, both, both, flat, flat, both, both, both, flat),
        out_specs=(both, both, both),
        check_vma=False,
    )
```

```python
import functools

import jax
import jax.numpy as jnp
from jax import lax
from jax.experimental import pallas as pl
from jax.experimental.pallas import tpu as pltpu
from jax.sharding import PartitionSpec as P


F32 = jnp.float32
BF16 = jnp.bfloat16
I32 = jnp.int32

STAR_DEV = 512
BLOCK = 128
STEP = 1.0
SOFT_STAR = 0.01
SOFT_GALAXY = 0.04

NT = (((1,), (1,)), ((), ()))
SMEM = pl.BlockSpec(memory_space=pltpu.SMEM)
VMEM = pl.BlockSpec(memory_space=pltpu.VMEM)
HBM = pl.BlockSpec(memory_space=pltpu.HBM)


def grant(mib):
    return pltpu.CompilerParams(vmem_limit_bytes=mib * 2**20)


def split3(x):
    a = x.astype(BF16).astype(F32)
    r = x - a
    b = r.astype(BF16).astype(F32)
    return a, b, r - b


def predicted(pos, vel, acc, jerk):
    half = 0.5 * STEP**2
    sixth = STEP**3 / 6.0
    return (
        pos + STEP * vel + half * acc + sixth * jerk,
        vel + STEP * acc + half * jerk,
    )


def chosen_hot(active_row, stars):
    row = lax.broadcasted_iota(I32, (stars, active_row.shape[1]), 0)
    return jnp.where(row == active_row, 1.0, 0.0).astype(BF16)


def sum_parts(x):
    n = x.shape[0] // 3
    return x[:n] + x[n : 2 * n] + x[2 * n : 3 * n]


def pre_kernel(pos_ref, vel_ref, acc_ref, jerk_ref, mass_ref, idx_ref, leaf_ref, block_ref,
               planes_ref, sent_ref, start_ref, hot_ref):
    nb = mass_ref.shape[0]
    lanes = lambda ref, q: jnp.concatenate([ref[q, b : b + 1, :] for b in range(nb)], 1)
    rows = lambda ref: jnp.concatenate([lanes(ref, q) for q in range(3)], 0)
    flat = lambda ref: jnp.concatenate([ref[b : b + 1, :] for b in range(ref.shape[0])], 1)
    pos, vel, acc, jerk = (rows(r) for r in (pos_ref, vel_ref, acc_ref, jerk_ref))
    x, v = predicted(pos, vel, acc, jerk)
    zero1 = jnp.zeros((1, pos.shape[1]), F32)
    planes_ref[...] = jnp.concatenate([x, v, flat(mass_ref), zero1], 0)
    hot = chosen_hot(idx_ref[...], pos.shape[1])
    hot_ref[...] = hot
    zero4 = jnp.zeros((4, pos.shape[1]), F32)
    parts = split3(jnp.concatenate([pos, vel, acc, jerk, zero4], 0))
    at = sum_parts(
        jnp.dot(jnp.concatenate(parts, 0).astype(BF16), hot, preferred_element_type=F32)
    )
    start_ref[...] = at
    ax, av = predicted(at[0:3], at[3:6], at[6:9], at[9:12])
    lists = [leaf_ref[...].astype(F32), block_ref[...].astype(F32)]
    targets = sent_ref.shape[0]
    lists.append(jnp.zeros((targets - 8, targets), F32))
    lists = jnp.concatenate(lists, 0).T
    active = jnp.concatenate([ax, av], 0)
    blank = jnp.zeros((1, active.shape[1]), F32)
    for e in range(targets):
        sent_ref[e] = jnp.concatenate([active, lists[e : e + 1, :], blank], 0)


def prepare(pos, vel, acc, jerk, mass, idx, leaf, block):
    stars = mass.size
    acts = idx.shape[1]
    return pl.pallas_call(
        pre_kernel,
        out_shape=(
            jax.ShapeDtypeStruct((8, stars), F32),
            jax.ShapeDtypeStruct((block.shape[1], 8, acts), F32),
            jax.ShapeDtypeStruct((16, acts), F32),
            jax.ShapeDtypeStruct((stars, acts), BF16),
        ),
    )(pos, vel, acc, jerk, mass, idx, leaf, block)


def pair_kernel(width, row_ref, act_ref, s0_ref, s1_ref, s2_ref, s3_ref, out_ref,
                rs_ref, b_ref, ws_ref):
    own = s0_ref.shape[1]
    refs = (s0_ref, s1_ref, s2_ref, s3_ref)
    n = own * len(refs)
    acts = act_ref.shape[2]
    ic = act_ref.shape[0] * acts

    @pl.when(pl.program_id(0) == 0)
    def _():
        for k, ref in enumerate(refs):
            s = ref[...]
            row = lax.broadcasted_iota(I32, s.shape, 0)
            s1, s2, s3 = split3(s)
            x = s[0:3]
            v = s[3:6]
            n1, n2, n3 = split3(jnp.sum(x * x, 0, keepdims=True))
            d1, d2, d3 = split3(jnp.sum(x * v, 0, keepdims=True))
            one = jnp.ones_like(n1)
            zero7 = jnp.zeros((7, own), F32)
            tail = [one, one, one, n1, n2, n3, d1, d2, d3, zero7]
            big = jnp.concatenate([s1, s2, s3, s1, s2, s1] + tail, 0)
            rs_ref[k * own : (k + 1) * own, :] = big.T.astype(BF16)
            m = s[6:7]
            g1, g2, g3 = split3(jnp.where(row == 6, m, s * m))
            b_ref[:, k * own : (k + 1) * own] = jnp.concatenate(
                [g1, g2, g3, jnp.zeros_like(g1)], 0
            ).astype(BF16)

    a = jnp.concatenate([act_ref[q] for q in range(act_ref.shape[0])], 1)
    x = a[0:3]
    v = a[3:6]
    zero2 = jnp.zeros((2, ic), F32)
    one = jnp.ones((1, ic), F32)
    zero3 = jnp.zeros((3, ic), F32)
    one3 = jnp.ones((3, ic), F32)
    zero7 = jnp.zeros((7, ic), F32)

    def left(p, extra, tail):
        p1, p2, p3 = split3(p)
        return jnp.concatenate(
            [p1, p1, p1, p2, p2, p3] + list(split3(extra)) + tail + [zero7], 0
        )

    lr = left(
        jnp.concatenate([-2.0 * x, zero3, zero2], 0),
        jnp.sum(x * x, 0, keepdims=True) + SOFT_STAR,
        [one3, zero3],
    )
    lv = left(
        jnp.concatenate([-v, -x, zero2], 0),
        jnp.sum(x * v, 0, keepdims=True),
        [zero3, one3],
    )
    L = jnp.concatenate([lr, lv], 1).astype(BF16)
    f = None
    for j0 in range(0, n, width):
        p = jnp.dot(rs_ref[j0 : j0 + width, :], L, preferred_element_type=F32)
        inv = lax.rsqrt(p[:, :ic])
        i2 = inv * inv
        w = i2 * inv
        ws_ref[j0 : j0 + width, :ic] = w.astype(BF16)
        ws_ref[j0 : j0 + width, ic:] = ((w * i2) * p[:, ic:]).astype(BF16)
        d = jnp.dot(
            b_ref[:, j0 : j0 + width],
            ws_ref[j0 : j0 + width, :],
            preferred_element_type=F32,
        )
        f = d if f is None else f + d
    t = sum_parts(f[0:24])
    wt = t[:, :ic]
    st = t[:, ic:]
    mw = wt[6:7]
    ms = st[6:7]
    acc = wt[0:3] - x * mw
    jerk = wt[3:6] - v * mw - 3.0 * (st[0:3] - x * ms)
    for q in range(act_ref.shape[0]):
        cut = slice(q * acts, (q + 1) * acts)
        out_ref[q] = jnp.concatenate([acc[:, cut], jerk[:, cut], zero2[:, cut]], 0)


def pair_terms(row, active, stars, cols, group=2, width=1024):
    acts = active.shape[2]
    own = stars[0].shape[1]
    n = own * len(stars)
    ic = group * acts
    steps = cols // group
    whole = pl.BlockSpec((8, own), lambda i, row: (0, 0))
    return pl.pallas_call(
        functools.partial(pair_kernel, width),
        grid_spec=pltpu.PrefetchScalarGridSpec(
            num_scalar_prefetch=1,
            grid=(steps,),
            in_specs=[
                pl.BlockSpec((group, 8, acts), lambda i, row: (row[0] * steps + i, 0, 0))
            ]
            + [whole] * len(stars),
            out_specs=pl.BlockSpec((group, 8, acts), lambda i, row: (i, 0, 0)),
            scratch_shapes=[
                pltpu.VMEM((n, 64), BF16),
                pltpu.VMEM((32, n), BF16),
                pltpu.VMEM((n, 2 * ic), BF16),
            ],
        ),
        out_shape=jax.ShapeDtypeStruct((cols, 8, acts), F32),
        compiler_params=grant(16),
        cost_estimate=pl.CostEstimate(
            flops=4 * 2 * 128 * cols * acts * n,
            transcendentals=cols * acts * n,
            bytes_accessed=4 * 2 * cols * 8 * acts,
        ),
    )(row, active, *stars)


def correct_kernel(part_ref, start_ref, planes_ref, hot_ref, pos_ref, mid_ref, send_ref):
    nb = pos_ref.shape[1]
    total = part_ref[0]
    for c in range(1, part_ref.shape[0]):
        total = total + part_ref[c]
    acc = total[0:3]
    jerk = total[3:6]
    x0, v0, a0, j0 = (start_ref[3 * q : 3 * q + 3, :] for q in range(4))
    v1 = v0 + (a0 + acc) * (0.5 * STEP) + (j0 - jerk) * (STEP**2 / 12.0)
    x1 = x0 + (v0 + v1) * (0.5 * STEP) + (a0 - acc) * (STEP**2 / 12.0)
    one = jnp.ones((2, x1.shape[1]), F32)
    parts = split3(jnp.concatenate([x1, v1, one], 0))
    planes = planes_ref[...]
    put = jnp.concatenate(parts + (jnp.zeros_like(parts[0]),), 0).astype(BF16)
    spread = sum_parts(
        lax.dot_general(put, hot_ref[...], NT, preferred_element_type=F32)[0:24]
    )
    new = jnp.where(spread[6:7] > 0.5, spread, planes)
    sent = []
    for b in range(nb):
        cut = slice(b * BLOCK, (b + 1) * BLOCK)
        for q in range(3):
            pos_ref[q, b : b + 1, :] = new[q : q + 1, cut]
            mid_ref[q, b : b + 1, :] = new[3 + q : 4 + q, cut]
        sent += [new[0:3, cut], planes[6:7, cut]]
    sent = jnp.concatenate(sent, 0)
    for e in range(send_ref.shape[0]):
        send_ref[e] = sent


def correct(part, start, planes, hot, nb, chips):
    return pl.pallas_call(
        correct_kernel,
        in_specs=[VMEM] * 4,
        out_shape=(
            jax.ShapeDtypeStruct((3, nb, BLOCK), F32),
            jax.ShapeDtypeStruct((3, nb, BLOCK), F32),
            jax.ShapeDtypeStruct((chips, 4 * nb, BLOCK), F32),
        ),
    )(part, start, planes, hot)


def target_terms(g):
    z1 = jnp.zeros((1, g.shape[1]), F32)
    z4 = jnp.zeros((4, g.shape[1]), F32)
    e = jnp.concatenate(split3(jnp.sum(g * g, 0, keepdims=True) + SOFT_GALAXY), 0)
    p1, p2, p3 = split3(-2.0 * g)
    low = []
    high = []
    for t in (p1, p1, p1, p2, p2, p3, jnp.ones_like(g), e):
        low += [t, z1, z4]
        high += [z4, t, z1]
    return jnp.concatenate(low + high, 0).T.astype(BF16)


def leaf_kernel(first, pos_ref, mass_ref, g_ref, lo_ref):
    z4 = jnp.zeros((4, 128), F32)

    def body(i, carry):
        l = first + i
        g = jnp.concatenate([pos_ref[q, pl.ds(l, 1), :] for q in range(3)], 0)
        g_ref[i] = target_terms(g)
        lo_ref[i] = jnp.concatenate([g, mass_ref[pl.ds(l, 1), :], z4], 0)
        return carry

    lax.fori_loop(0, g_ref.shape[0], body, 0, unroll=4)


def leaf_prep(pos, mass, part, parts):
    nl = mass.shape[0] // parts
    return pl.pallas_call(
        functools.partial(leaf_kernel, part * nl),
        out_shape=(
            jax.ShapeDtypeStruct((nl, 128, 128), BF16),
            jax.ShapeDtypeStruct((nl, 8, 128), F32),
        ),
        cost_estimate=pl.CostEstimate(
            flops=10**7, transcendentals=0, bytes_accessed=3 * 10**6
        ),
    )(pos, mass)


def gathered(parts, into, sems):
    n = parts[0].shape[0]
    return [
        pltpu.make_async_copy(p, into.at[i * n : (i + 1) * n], sems.at[i])
        for i, p in enumerate(parts)
    ]


def fetch_kernel(arrived_ref, far_ref, out_ref, table_ref, lo_ref, tab_ref, sems):
    nl = far_ref.shape[0]
    n = out_ref.shape[0]
    first = pl.program_id(0) * n

    @pl.when(pl.program_id(0) == 0)
    def _():
        leaves = pltpu.make_async_copy(far_ref, lo_ref.at[0:nl], sems.at[0])
        leaves.start()
        t = arrived_ref[:, 6, :].T[0:8, :].astype(I32)
        table_ref[...] = jnp.where(t < 0, nl, t)
        numbers = pltpu.make_async_copy(table_ref, tab_ref, sems.at[1])
        numbers.start()
        lo_ref[nl] = jnp.zeros((8, 128), F32)
        numbers.wait()
        leaves.wait()

    def body(d, carry):
        for h in range(2):
            a = lo_ref[tab_ref[2 * h, first + d]]
            b = lo_ref[tab_ref[2 * h + 1, first + d]]
            out_ref[d, 8 * h : 8 * h + 8, :] = a + pltpu.roll(b, 4, 0)
        return carry

    lax.fori_loop(0, n, body, 0, unroll=8)


def fetch(arrived, lo, steps=4):
    nl = lo.shape[0]
    devices = arrived.shape[0]
    n = devices // steps
    return pl.pallas_call(
        fetch_kernel,
        grid=(steps,),
        in_specs=[pl.BlockSpec(arrived.shape, lambda i: (0, 0, 0)), HBM],
        out_specs=(
            pl.BlockSpec((n, 16, 128), lambda i: (i, 0, 0)),
            pl.BlockSpec((8, devices), lambda i: (0, 0)),
        ),
        out_shape=(
            jax.ShapeDtypeStruct((devices, 16, 128), F32),
            jax.ShapeDtypeStruct((8, devices), I32),
        ),
        compiler_params=grant(53),
        scratch_shapes=[
            pltpu.VMEM((nl + 1, 8, 128), F32),
            pltpu.SMEM((8, devices), I32),
            pltpu.SemaphoreType.DMA((2,)),
        ],
    )(arrived, lo)


def attract(G, ng, fine, bodies, targets, ready, g_ref, acc_ref, t_ref, s_ref, v_ref):
    acc_ref[...] = jnp.zeros_like(acc_ref)
    r8 = lax.broadcasted_iota(I32, (8, 128), 0)
    low = r8 < 4
    q4 = r8 & 3
    one = jnp.ones((8, 128), F32)
    zero8 = jnp.zeros((8, 128), F32)
    zero64 = jnp.zeros((64, 128), BF16)

    def prep(g, b, j):
        s = bodies(g, j, low)
        s1, s2, s3 = split3(s)
        x2 = jnp.where(q4 == 3, 0.0, s * s)
        x2 = x2 + jnp.where((r8 & 1) == 0, pltpu.roll(x2, 7, 0), pltpu.roll(x2, 1, 0))
        x2 = x2 + jnp.where((r8 & 2) == 0, pltpu.roll(x2, 6, 0), pltpu.roll(x2, 2, 0))
        n1, n2, n3 = split3(x2)
        t1 = jnp.where(q4 == 0, n1, jnp.where(q4 == 1, n2, n3))
        m = jnp.where(
            low,
            jnp.broadcast_to(s[3:4], (8, 128)),
            jnp.broadcast_to(s[7:8], (8, 128)),
        )
        for q, t in enumerate((s1, s2, s3, t1)):
            t_ref[b, j, 8 * q : 8 * q + 8, :] = t
        for q, t in enumerate(split3(jnp.where(q4 == 3, s, s * m))):
            s_ref[b, j, 8 * q : 8 * q + 8, :] = t

    def force(g, b, j):
        la, lb = targets(g, j)
        lane = lax.broadcasted_iota(I32, (128, 128), 1)
        L = jnp.where(lane < 64, g_ref[la], g_ref[lb])
        s1, s2, s3, t1 = (t_ref[b, j, 8 * q : 8 * q + 8, :] for q in range(4))
        T = jnp.concatenate([s1, s2, s3, s1, s2, s1, t1, one], 0).astype(BF16)
        W = jnp.concatenate(
            [jnp.concatenate([T, zero64], 1), jnp.concatenate([zero64, T], 1)], 0
        )
        inv = lax.rsqrt(jnp.dot(L, W, preferred_element_type=F32))
        v_ref[b, j] = inv * inv * inv

    def sums(g, b, j):
        S = jnp.concatenate([s_ref[b, j], zero8], 0).astype(BF16)
        u = v_ref[b, j]
        hi = u.astype(BF16)
        if fine:
            lo = (u - hi.astype(F32)).astype(BF16)
            S = jnp.concatenate([S, S], 1)
            V = [jnp.concatenate([t[:, :128] for t in (hi, lo)], 1)]
            V.append(jnp.concatenate([t[:, 128:] for t in (hi, lo)], 1))
        else:
            V = [hi[:, :128], hi[:, 128:]]
        f = lax.dot_general(S, jnp.concatenate(V, 0), NT, preferred_element_type=F32)
        return targets(g, j) + (sum_parts(f[0:24]),)

    def step(g, b, more, more2):
        done = []
        for j in range(G):
            done.append(sums(g, b, j))
            if more:
                force(g + 1, 1 - b, j)
            if more2:
                prep(g + 2, b, j)
        for la, lb, t in done:
            acc_ref[la] += jnp.where(low, t[:, :128], 0.0)
            acc_ref[lb] += jnp.where(low, 0.0, t[:, 128:])

    for j in range(G):
        prep(0, 0, j)
        prep(1, 1, j)
    ready()
    for j in range(G):
        force(0, 0, j)

    def body(i, carry):
        step(2 * i, 0, True, True)
        step(2 * i + 1, 1, True, True)
        return carry

    lax.fori_loop(0, ng // 2 - 1, body, 0)
    step(ng - 2, 0, True, False)
    step(ng - 1, 1, False, False)


def attract_scratch(targets, G):
    return [
        pltpu.VMEM((targets, 8, 128), F32),
        pltpu.VMEM((2, G, 32, 128), F32),
        pltpu.VMEM((2, G, 24, 128), F32),
        pltpu.VMEM((2, G, 128, 256), F32),
    ]


def attract_cost(entries):
    return pl.CostEstimate(
        flops=3 * 2 * entries * 128**3,
        transcendentals=entries * 128**2,
        bytes_accessed=entries * 4 * 512,
    )


def kick_kernel(G, block_ref, leaf_ref, pos_ref, mid_ref, vel_ref, g_ref, *scratch):
    nb = pos_ref.shape[1]
    acc_ref = scratch[0]
    place = [
        jnp.concatenate([pos_ref[q, b : b + 1, :] for q in range(3)], 0) for b in range(nb)
    ]
    for b in range(nb):
        g_ref[b] = target_terms(place[b])

    def where(g, j):
        e = g * (G // 2) + j // 2
        h = 2 * (j % 2)
        return jnp.maximum(block_ref[h, e], 0), jnp.maximum(block_ref[h + 1, e], 0)

    def bodies(g, j, low):
        h = 8 * (j % 2)
        return leaf_ref[g * (G // 2) + j // 2, h : h + 8, :]

    attract(G, 2 * leaf_ref.shape[0] // G, False, bodies, where, lambda: None, g_ref, *scratch)
    for b in range(nb):
        a = acc_ref[b]
        a = a[0:4] + a[4:8]
        kick = a[0:3] - place[b] * a[3:4]
        for q in range(3):
            vel_ref[q, b : b + 1, :] = mid_ref[q, b : b + 1, :] + STEP * kick[q : q + 1]


def kicks(block, leaves, pos, mid, G=16):
    nb = pos.shape[1]
    return pl.pallas_call(
        functools.partial(kick_kernel, G),
        in_specs=[SMEM] + [VMEM] * 3,
        out_shape=jax.ShapeDtypeStruct(mid.shape, F32),
        scratch_shapes=[pltpu.VMEM((nb, 128, 128), BF16)] + attract_scratch(nb, G),
        cost_estimate=attract_cost(4 * leaves.shape[0]),
    )(block, leaves, pos, mid)


def pull_kernel(G, scale, nparts, core_ref, tab_ref, own_ref, other_ref, *refs):
    parts = refs[:nparts]
    far_ref, pull_ref, g_ref, gpos_ref, sems = refs[nparts : nparts + 5]
    scratch = refs[nparts + 5 :]
    acc_ref = scratch[0]
    core = core_ref[0]
    copies = gathered(parts, g_ref, sems)
    copies.append(pltpu.make_async_copy(far_ref, gpos_ref, sems.at[nparts]))
    for copy in copies:
        copy.start()

    def ready():
        for copy in copies:
            copy.wait()

    def source(g, j):
        i = g * (G // 4) + j // 4
        flip = (j // 2) % 2
        return (own_ref, other_ref)[flip], i, 2 * i + (core ^ flip), 2 * (j % 2)

    def where(g, j):
        _, _, d, h = source(g, j)
        last = g_ref.shape[0] - 1
        return jnp.minimum(tab_ref[h, d], last), jnp.minimum(tab_ref[h + 1, d], last)

    def bodies(g, j, low):
        ref, i, d, h = source(g, j)
        a = tab_ref[4 + h, d]
        b = tab_ref[5 + h, d]
        ta = ref[i, lax.shift_right_logical(a, 1) & 1]
        tb = ref[i, lax.shift_right_logical(b, 1) & 1]
        ta = jnp.where((a & 1) == 1, pltpu.roll(ta, 4, 0), ta)
        tb = jnp.where((b & 1) == 1, tb, pltpu.roll(tb, 4, 0))
        return jnp.where(jnp.where(low, a, b) > 3, 0.0, jnp.where(low, ta, tb))

    ng = 4 * own_ref.shape[0] // G
    attract(G, ng, True, bodies, where, ready, g_ref, *scratch)

    def finish(l, carry):
        a = acc_ref[l]
        a = a[0:4] + a[4:8]
        for q in range(3):
            g = gpos_ref[q, pl.ds(l, 1), :]
            pull_ref[q, pl.ds(l, 1), :] = (a[q : q + 1] - g * a[3:4]) * scale
        return carry

    lax.fori_loop(0, g_ref.shape[0], finish, 0, unroll=8)


def pulls(core, table, own, other, parts, gpos, scale, G=16):
    nl = gpos.shape[1]
    return pl.pallas_call(
        functools.partial(pull_kernel, G, scale, len(parts)),
        in_specs=[SMEM] * 2 + [VMEM] * 2 + [HBM] * (len(parts) + 1),
        out_shape=jax.ShapeDtypeStruct((3, nl, 128), F32),
        compiler_params=grant(51),
        scratch_shapes=[
            pltpu.VMEM((nl, 128, 128), BF16),
            pltpu.VMEM(gpos.shape, F32),
            pltpu.SemaphoreType.DMA((len(parts) + 1,)),
        ]
        + attract_scratch(nl, G),
        cost_estimate=attract_cost(8 * own.shape[0]),
    )(core, table, own, other, *parts, gpos)


def local(
    star_pos,
    star_vel,
    star_acc,
    star_jerk,
    star_mass,
    active_index,
    send_block,
    send_leaf,
    galaxy_pos,
    galaxy_mass,
):
    rows = lax.axis_size("row")
    cols = lax.axis_size("col")
    devices = rows * cols
    nb = star_pos.shape[0]
    both = ("row", "col")
    turn = lambda x: x.transpose(1, 0, 2)
    row = lax.axis_index("row").astype(I32).reshape(1)
    core = (lax.axis_index("col") & 1).astype(I32).reshape(1)
    block = send_block[0].T
    gpos = turn(galaxy_pos)
    planes, sent, start, hot = prepare(
        turn(star_pos), turn(star_vel), turn(star_acc), turn(star_jerk),
        star_mass, active_index, send_leaf[0].T, block,
    )
    arrived = lax.all_to_all(sent, both, 0, 0, tiled=True)
    stars = [planes]
    for k in range(1, rows):
        perm = [(i, (i + k) % rows) for i in range(rows)]
        stars.append(lax.ppermute(planes, "row", perm))
    g, lo = leaf_prep(gpos, galaxy_mass, 0, 1)
    leaves, table = fetch(arrived, lo)
    leaves = lax.all_to_all(leaves, both, 0, 0, tiled=True)
    parts = pair_terms(row, arrived, stars, cols)
    parts = lax.all_to_all(parts, "col", 0, 0, tiled=True)
    pos_new, mid, outgoing = correct(parts, start, planes, hot, nb, devices // 2)
    same_core = [[d for d in range(devices) if d % 2 == c] for c in range(2)]
    own = lax.all_to_all(outgoing, both, 0, 0, tiled=True, axis_index_groups=same_core)
    other = lax.ppermute(own, "col", [(i, i ^ 1) for i in range(cols)])
    vel_new = kicks(block, leaves, pos_new, mid)
    tiles = lambda x: x.reshape(-1, 2, 8, BLOCK)
    scale = STAR_DEV * devices / BLOCK
    pull = pulls(
        core, table, tiles(own), tiles(other), [g], gpos, scale
    )
    return turn(pos_new), turn(vel_new), turn(pull)


def solution(mesh):
    both = P(("row", "col"), None, None)
    flat = P(("row", "col"), None)
    return jax.shard_map(
        local,
        mesh=mesh,
        in_specs=(both, both, both, both, flat, flat, both, both, both, flat),
        out_specs=(both, both, both),
        check_vma=False,
    )
```

```python
import functools

import jax
import jax.numpy as jnp
from jax import lax
from jax.experimental import pallas as pl
from jax.experimental.pallas import tpu as pltpu
from jax.sharding import PartitionSpec as P


F32 = jnp.float32
BF16 = jnp.bfloat16
I32 = jnp.int32

STAR_DEV = 512
BLOCK = 128
STEP = 1.0
SOFT_STAR = 0.01
SOFT_GALAXY = 0.04

NT = (((1,), (1,)), ((), ()))
SMEM = pl.BlockSpec(memory_space=pltpu.SMEM)
VMEM = pl.BlockSpec(memory_space=pltpu.VMEM)
HBM = pl.BlockSpec(memory_space=pltpu.HBM)


def grant(mib):
    return pltpu.CompilerParams(vmem_limit_bytes=mib * 2**20)


def split3(x):
    a = x.astype(BF16).astype(F32)
    r = x - a
    b = r.astype(BF16).astype(F32)
    return a, b, r - b


def spread_scales(shape):
    lane = lax.broadcasted_iota(I32, shape, 1) & 63
    c = 1.0 + lane.astype(F32) * (1.0 / 128.0)
    return c, c * c * lax.rsqrt(c)


def predicted(pos, vel, acc, jerk):
    half = 0.5 * STEP**2
    sixth = STEP**3 / 6.0
    return (
        pos + STEP * vel + half * acc + sixth * jerk,
        vel + STEP * acc + half * jerk,
    )


def chosen_hot(active_row, stars):
    row = lax.broadcasted_iota(I32, (stars, active_row.shape[1]), 0)
    return jnp.where(row == active_row, 1.0, 0.0).astype(BF16)


def sum_parts(x):
    n = x.shape[0] // 3
    return x[:n] + x[n : 2 * n] + x[2 * n : 3 * n]


def pre_kernel(pos_ref, vel_ref, acc_ref, jerk_ref, mass_ref, idx_ref, leaf_ref, block_ref,
               planes_ref, sent_ref, start_ref, hot_ref):
    nb = mass_ref.shape[0]
    lanes = lambda ref, q: jnp.concatenate([ref[q, b : b + 1, :] for b in range(nb)], 1)
    rows = lambda ref: jnp.concatenate([lanes(ref, q) for q in range(3)], 0)
    flat = lambda ref: jnp.concatenate([ref[b : b + 1, :] for b in range(ref.shape[0])], 1)
    pos, vel, acc, jerk = (rows(r) for r in (pos_ref, vel_ref, acc_ref, jerk_ref))
    x, v = predicted(pos, vel, acc, jerk)
    zero1 = jnp.zeros((1, pos.shape[1]), F32)
    planes_ref[...] = jnp.concatenate([x, v, flat(mass_ref), zero1], 0)
    hot = chosen_hot(idx_ref[...], pos.shape[1])
    hot_ref[...] = hot
    zero4 = jnp.zeros((4, pos.shape[1]), F32)
    parts = split3(jnp.concatenate([pos, vel, acc, jerk, zero4], 0))
    at = sum_parts(
        jnp.dot(jnp.concatenate(parts, 0).astype(BF16), hot, preferred_element_type=F32)
    )
    start_ref[...] = at
    ax, av = predicted(at[0:3], at[3:6], at[6:9], at[9:12])
    lists = [leaf_ref[...].astype(F32), block_ref[...].astype(F32)]
    targets = sent_ref.shape[0]
    lists.append(jnp.zeros((targets - 8, targets), F32))
    lists = jnp.concatenate(lists, 0).T
    active = jnp.concatenate([ax, av], 0)
    blank = jnp.zeros((1, active.shape[1]), F32)
    for e in range(targets):
        sent_ref[e] = jnp.concatenate([active, lists[e : e + 1, :], blank], 0)


def prepare(pos, vel, acc, jerk, mass, idx, leaf, block):
    stars = mass.size
    acts = idx.shape[1]
    return pl.pallas_call(
        pre_kernel,
        out_shape=(
            jax.ShapeDtypeStruct((8, stars), F32),
            jax.ShapeDtypeStruct((block.shape[1], 8, acts), F32),
            jax.ShapeDtypeStruct((16, acts), F32),
            jax.ShapeDtypeStruct((stars, acts), BF16),
        ),
    )(pos, vel, acc, jerk, mass, idx, leaf, block)


def pair_kernel(width, row_ref, act_ref, s0_ref, s1_ref, s2_ref, s3_ref, out_ref,
                rs_ref, b_ref, ws_ref):
    own = s0_ref.shape[1]
    refs = (s0_ref, s1_ref, s2_ref, s3_ref)
    n = own * len(refs)
    acts = act_ref.shape[2]
    ic = act_ref.shape[0] * acts

    @pl.when(pl.program_id(0) == 0)
    def _():
        for k, ref in enumerate(refs):
            s = ref[...]
            row = lax.broadcasted_iota(I32, s.shape, 0)
            scale, back = spread_scales(s.shape)
            s1, s2, s3 = split3(s * scale)
            x = s[0:3]
            v = s[3:6]
            one = scale[0:1]
            n1, n2, n3 = split3(jnp.sum(x * x, 0, keepdims=True) * one)
            d1, d2, d3 = split3(jnp.sum(x * v, 0, keepdims=True) * one)
            zero7 = jnp.zeros((7, own), F32)
            tail = [one, one, one, n1, n2, n3, d1, d2, d3, zero7]
            big = jnp.concatenate([s1, s2, s3, s1, s2, s1] + tail, 0)
            rs_ref[k * own : (k + 1) * own, :] = big.T.astype(BF16)
            m = s[6:7]
            g1, g2, g3 = split3(jnp.where(row == 6, m, s * m) * back)
            b_ref[:, k * own : (k + 1) * own] = jnp.concatenate(
                [g1, g2, g3, jnp.zeros_like(g1)], 0
            ).astype(BF16)

    a = jnp.concatenate([act_ref[q] for q in range(act_ref.shape[0])], 1)
    x = a[0:3]
    v = a[3:6]
    zero2 = jnp.zeros((2, ic), F32)
    one = jnp.ones((1, ic), F32)
    zero3 = jnp.zeros((3, ic), F32)
    one3 = jnp.ones((3, ic), F32)
    zero7 = jnp.zeros((7, ic), F32)

    def left(p, extra, tail):
        p1, p2, p3 = split3(p)
        return jnp.concatenate(
            [p1, p1, p1, p2, p2, p3] + list(split3(extra)) + tail + [zero7], 0
        )

    lr = left(
        jnp.concatenate([-2.0 * x, zero3, zero2], 0),
        jnp.sum(x * x, 0, keepdims=True) + SOFT_STAR,
        [one3, zero3],
    )
    lv = left(
        jnp.concatenate([-v, -x, zero2], 0),
        jnp.sum(x * v, 0, keepdims=True),
        [zero3, one3],
    )
    L = jnp.concatenate([lr, lv], 1).astype(BF16)
    f = None
    for j0 in range(0, n, width):
        p = jnp.dot(rs_ref[j0 : j0 + width, :], L, preferred_element_type=F32)
        inv = lax.rsqrt(p[:, :ic])
        i2 = inv * inv
        w = i2 * inv
        ws_ref[j0 : j0 + width, :ic] = w.astype(BF16)
        ws_ref[j0 : j0 + width, ic:] = ((w * i2) * p[:, ic:]).astype(BF16)
        d = jnp.dot(
            b_ref[:, j0 : j0 + width],
            ws_ref[j0 : j0 + width, :],
            preferred_element_type=F32,
        )
        f = d if f is None else f + d
    t = sum_parts(f[0:24])
    wt = t[:, :ic]
    st = t[:, ic:]
    mw = wt[6:7]
    ms = st[6:7]
    acc = wt[0:3] - x * mw
    jerk = wt[3:6] - v * mw - 3.0 * (st[0:3] - x * ms)
    for q in range(act_ref.shape[0]):
        cut = slice(q * acts, (q + 1) * acts)
        out_ref[q] = jnp.concatenate([acc[:, cut], jerk[:, cut], zero2[:, cut]], 0)


def pair_terms(row, active, stars, cols, group=2, width=1024):
    acts = active.shape[2]
    own = stars[0].shape[1]
    n = own * len(stars)
    ic = group * acts
    steps = cols // group
    whole = pl.BlockSpec((8, own), lambda i, row: (0, 0))
    return pl.pallas_call(
        functools.partial(pair_kernel, width),
        grid_spec=pltpu.PrefetchScalarGridSpec(
            num_scalar_prefetch=1,
            grid=(steps,),
            in_specs=[
                pl.BlockSpec((group, 8, acts), lambda i, row: (row[0] * steps + i, 0, 0))
            ]
            + [whole] * len(stars),
            out_specs=pl.BlockSpec((group, 8, acts), lambda i, row: (i, 0, 0)),
            scratch_shapes=[
                pltpu.VMEM((n, 64), BF16),
                pltpu.VMEM((32, n), BF16),
                pltpu.VMEM((n, 2 * ic), BF16),
            ],
        ),
        out_shape=jax.ShapeDtypeStruct((cols, 8, acts), F32),
        compiler_params=grant(16),
        cost_estimate=pl.CostEstimate(
            flops=4 * 2 * 128 * cols * acts * n,
            transcendentals=cols * acts * n,
            bytes_accessed=4 * 2 * cols * 8 * acts,
        ),
    )(row, active, *stars)


def correct_kernel(part_ref, start_ref, planes_ref, hot_ref, pos_ref, mid_ref, send_ref):
    nb = pos_ref.shape[1]
    total = part_ref[0]
    for c in range(1, part_ref.shape[0]):
        total = total + part_ref[c]
    acc = total[0:3]
    jerk = total[3:6]
    x0, v0, a0, j0 = (start_ref[3 * q : 3 * q + 3, :] for q in range(4))
    v1 = v0 + (a0 + acc) * (0.5 * STEP) + (j0 - jerk) * (STEP**2 / 12.0)
    x1 = x0 + (v0 + v1) * (0.5 * STEP) + (a0 - acc) * (STEP**2 / 12.0)
    one = jnp.ones((2, x1.shape[1]), F32)
    parts = split3(jnp.concatenate([x1, v1, one], 0))
    planes = planes_ref[...]
    put = jnp.concatenate(parts + (jnp.zeros_like(parts[0]),), 0).astype(BF16)
    spread = sum_parts(
        lax.dot_general(put, hot_ref[...], NT, preferred_element_type=F32)[0:24]
    )
    new = jnp.where(spread[6:7] > 0.5, spread, planes)
    sent = []
    for b in range(nb):
        cut = slice(b * BLOCK, (b + 1) * BLOCK)
        for q in range(3):
            pos_ref[q, b : b + 1, :] = new[q : q + 1, cut]
            mid_ref[q, b : b + 1, :] = new[3 + q : 4 + q, cut]
        sent += [new[0:3, cut], planes[6:7, cut]]
    sent = jnp.concatenate(sent, 0)
    for e in range(send_ref.shape[0]):
        send_ref[e] = sent


def correct(part, start, planes, hot, nb, chips):
    return pl.pallas_call(
        correct_kernel,
        in_specs=[VMEM] * 4,
        out_shape=(
            jax.ShapeDtypeStruct((3, nb, BLOCK), F32),
            jax.ShapeDtypeStruct((3, nb, BLOCK), F32),
            jax.ShapeDtypeStruct((chips, 4 * nb, BLOCK), F32),
        ),
    )(part, start, planes, hot)


def target_terms(g):
    z1 = jnp.zeros((1, g.shape[1]), F32)
    z4 = jnp.zeros((4, g.shape[1]), F32)
    e = jnp.concatenate(split3(jnp.sum(g * g, 0, keepdims=True) + SOFT_GALAXY), 0)
    p1, p2, p3 = split3(-2.0 * g)
    low = []
    high = []
    for t in (p1, p1, p1, p2, p2, p3, jnp.ones_like(g), e):
        low += [t, z1, z4]
        high += [z4, t, z1]
    return jnp.concatenate(low + high, 0).T.astype(BF16)


def leaf_kernel(first, pos_ref, mass_ref, g_ref, lo_ref):
    z4 = jnp.zeros((4, 128), F32)

    def body(i, carry):
        l = first + i
        g = jnp.concatenate([pos_ref[q, pl.ds(l, 1), :] for q in range(3)], 0)
        g_ref[i] = target_terms(g)
        lo_ref[i] = jnp.concatenate([g, mass_ref[pl.ds(l, 1), :], z4], 0)
        return carry

    lax.fori_loop(0, g_ref.shape[0], body, 0, unroll=4)


def leaf_prep(pos, mass, part, parts):
    nl = mass.shape[0] // parts
    return pl.pallas_call(
        functools.partial(leaf_kernel, part * nl),
        out_shape=(
            jax.ShapeDtypeStruct((nl, 128, 128), BF16),
            jax.ShapeDtypeStruct((nl, 8, 128), F32),
        ),
        cost_estimate=pl.CostEstimate(
            flops=10**7, transcendentals=0, bytes_accessed=3 * 10**6
        ),
    )(pos, mass)


def gathered(parts, into, sems):
    n = parts[0].shape[0]
    return [
        pltpu.make_async_copy(p, into.at[i * n : (i + 1) * n], sems.at[i])
        for i, p in enumerate(parts)
    ]


def fetch_kernel(arrived_ref, far_ref, out_ref, table_ref, lo_ref, tab_ref, sems):
    nl = far_ref.shape[0]
    n = out_ref.shape[0]
    first = pl.program_id(0) * n

    @pl.when(pl.program_id(0) == 0)
    def _():
        leaves = pltpu.make_async_copy(far_ref, lo_ref.at[0:nl], sems.at[0])
        leaves.start()
        t = arrived_ref[:, 6, :].T[0:8, :].astype(I32)
        table_ref[...] = jnp.where(t < 0, nl, t)
        numbers = pltpu.make_async_copy(table_ref, tab_ref, sems.at[1])
        numbers.start()
        lo_ref[nl] = jnp.zeros((8, 128), F32)
        numbers.wait()
        leaves.wait()

    def body(d, carry):
        for h in range(2):
            a = lo_ref[tab_ref[2 * h, first + d]]
            b = lo_ref[tab_ref[2 * h + 1, first + d]]
            out_ref[d, 8 * h : 8 * h + 8, :] = a + pltpu.roll(b, 4, 0)
        return carry

    lax.fori_loop(0, n, body, 0, unroll=8)


def fetch(arrived, lo, steps=2):
    nl = lo.shape[0]
    devices = arrived.shape[0]
    n = devices // steps
    return pl.pallas_call(
        fetch_kernel,
        grid=(steps,),
        in_specs=[pl.BlockSpec(arrived.shape, lambda i: (0, 0, 0)), HBM],
        out_specs=(
            pl.BlockSpec((n, 16, 128), lambda i: (i, 0, 0)),
            pl.BlockSpec((8, devices), lambda i: (0, 0)),
        ),
        out_shape=(
            jax.ShapeDtypeStruct((devices, 16, 128), F32),
            jax.ShapeDtypeStruct((8, devices), I32),
        ),
        compiler_params=grant(53),
        scratch_shapes=[
            pltpu.VMEM((nl + 1, 8, 128), F32),
            pltpu.SMEM((8, devices), I32),
            pltpu.SemaphoreType.DMA((2,)),
        ],
    )(arrived, lo)


def attract(G, ng, fine, bodies, targets, ready, g_ref, acc_ref, t_ref, s_ref, v_ref):
    acc_ref[...] = jnp.zeros_like(acc_ref)
    r8 = lax.broadcasted_iota(I32, (8, 128), 0)
    low = r8 < 4
    q4 = r8 & 3
    one, back = (jnp.ones((8, 128), F32),) * 2 if fine else spread_scales((8, 128))
    zero8 = jnp.zeros((8, 128), F32)
    zero64 = jnp.zeros((64, 128), BF16)

    def prep(g, b, j):
        s = bodies(g, j, low)
        s1, s2, s3 = split3(s if fine else s * one)
        x2 = jnp.where(q4 == 3, 0.0, s * s)
        x2 = x2 + jnp.where((r8 & 1) == 0, pltpu.roll(x2, 7, 0), pltpu.roll(x2, 1, 0))
        x2 = x2 + jnp.where((r8 & 2) == 0, pltpu.roll(x2, 6, 0), pltpu.roll(x2, 2, 0))
        n1, n2, n3 = split3(x2 if fine else x2 * one)
        t1 = jnp.where(q4 == 0, n1, jnp.where(q4 == 1, n2, n3))
        m = jnp.where(
            low,
            jnp.broadcast_to(s[3:4], (8, 128)),
            jnp.broadcast_to(s[7:8], (8, 128)),
        )
        for q, t in enumerate((s1, s2, s3, t1)):
            t_ref[b, j, 8 * q : 8 * q + 8, :] = t
        weighted = jnp.where(q4 == 3, s, s * m)
        for q, t in enumerate(split3(weighted if fine else weighted * back)):
            s_ref[b, j, 8 * q : 8 * q + 8, :] = t

    def force(g, b, j):
        la, lb = targets(g, j)
        lane = lax.broadcasted_iota(I32, (128, 128), 1)
        L = jnp.where(lane < 64, g_ref[la], g_ref[lb])
        s1, s2, s3, t1 = (t_ref[b, j, 8 * q : 8 * q + 8, :] for q in range(4))
        T = jnp.concatenate([s1, s2, s3, s1, s2, s1, t1, one], 0).astype(BF16)
        W = jnp.concatenate(
            [jnp.concatenate([T, zero64], 1), jnp.concatenate([zero64, T], 1)], 0
        )
        inv = lax.rsqrt(jnp.dot(L, W, preferred_element_type=F32))
        v_ref[b, j] = inv * inv * inv

    def sums(g, b, j):
        S = jnp.concatenate([s_ref[b, j], zero8], 0).astype(BF16)
        u = v_ref[b, j]
        hi = u.astype(BF16)
        if fine:
            lo = (u - hi.astype(F32)).astype(BF16)
            S = jnp.concatenate([S, S], 1)
            V = [jnp.concatenate([t[:, :128] for t in (hi, lo)], 1)]
            V.append(jnp.concatenate([t[:, 128:] for t in (hi, lo)], 1))
        else:
            V = [hi[:, :128], hi[:, 128:]]
        f = lax.dot_general(S, jnp.concatenate(V, 0), NT, preferred_element_type=F32)
        return targets(g, j) + (sum_parts(f[0:24]),)

    def step(g, b, more, more2):
        done = []
        for j in range(G):
            done.append(sums(g, b, j))
            if more:
                force(g + 1, 1 - b, j)
            if more2:
                prep(g + 2, b, j)
        for la, lb, t in done:
            acc_ref[la] += jnp.where(low, t[:, :128], 0.0)
            acc_ref[lb] += jnp.where(low, 0.0, t[:, 128:])

    for j in range(G):
        prep(0, 0, j)
        prep(1, 1, j)
    ready()
    for j in range(G):
        force(0, 0, j)

    def body(i, carry):
        step(2 * i, 0, True, True)
        step(2 * i + 1, 1, True, True)
        return carry

    lax.fori_loop(0, ng // 2 - 1, body, 0)
    step(ng - 2, 0, True, False)
    step(ng - 1, 1, False, False)


def attract_scratch(targets, G):
    return [
        pltpu.VMEM((targets, 8, 128), F32),
        pltpu.VMEM((2, G, 32, 128), F32),
        pltpu.VMEM((2, G, 24, 128), F32),
        pltpu.VMEM((2, G, 128, 256), F32),
    ]


def attract_cost(entries):
    return pl.CostEstimate(
        flops=3 * 2 * entries * 128**3,
        transcendentals=entries * 128**2,
        bytes_accessed=entries * 4 * 512,
    )


def kick_kernel(G, block_ref, leaf_ref, pos_ref, mid_ref, vel_ref, g_ref, *scratch):
    nb = pos_ref.shape[1]
    acc_ref = scratch[0]
    place = [
        jnp.concatenate([pos_ref[q, b : b + 1, :] for q in range(3)], 0) for b in range(nb)
    ]
    for b in range(nb):
        g_ref[b] = target_terms(place[b])

    def where(g, j):
        e = g * (G // 2) + j // 2
        h = 2 * (j % 2)
        return jnp.maximum(block_ref[h, e], 0), jnp.maximum(block_ref[h + 1, e], 0)

    def bodies(g, j, low):
        h = 8 * (j % 2)
        return leaf_ref[g * (G // 2) + j // 2, h : h + 8, :]

    attract(G, 2 * leaf_ref.shape[0] // G, False, bodies, where, lambda: None, g_ref, *scratch)
    for b in range(nb):
        a = acc_ref[b]
        a = a[0:4] + a[4:8]
        kick = a[0:3] - place[b] * a[3:4]
        for q in range(3):
            vel_ref[q, b : b + 1, :] = mid_ref[q, b : b + 1, :] + STEP * kick[q : q + 1]


def kicks(block, leaves, pos, mid, G=16):
    nb = pos.shape[1]
    return pl.pallas_call(
        functools.partial(kick_kernel, G),
        in_specs=[SMEM] + [VMEM] * 3,
        out_shape=jax.ShapeDtypeStruct(mid.shape, F32),
        scratch_shapes=[pltpu.VMEM((nb, 128, 128), BF16)] + attract_scratch(nb, G),
        cost_estimate=attract_cost(4 * leaves.shape[0]),
    )(block, leaves, pos, mid)


def pull_kernel(G, scale, nparts, core_ref, tab_ref, own_ref, other_ref, *refs):
    parts = refs[:nparts]
    far_ref, pull_ref, g_ref, gpos_ref, sems = refs[nparts : nparts + 5]
    scratch = refs[nparts + 5 :]
    acc_ref = scratch[0]
    core = core_ref[0]
    copies = gathered(parts, g_ref, sems)
    copies.append(pltpu.make_async_copy(far_ref, gpos_ref, sems.at[nparts]))
    for copy in copies:
        copy.start()

    def ready():
        for copy in copies:
            copy.wait()

    def source(g, j):
        i = g * (G // 4) + j // 4
        flip = (j // 2) % 2
        return (own_ref, other_ref)[flip], i, 2 * i + (core ^ flip), 2 * (j % 2)

    def where(g, j):
        _, _, d, h = source(g, j)
        last = g_ref.shape[0] - 1
        return jnp.minimum(tab_ref[h, d], last), jnp.minimum(tab_ref[h + 1, d], last)

    def bodies(g, j, low):
        ref, i, d, h = source(g, j)
        a = tab_ref[4 + h, d]
        b = tab_ref[5 + h, d]
        ta = ref[i, lax.shift_right_logical(a, 1) & 1]
        tb = ref[i, lax.shift_right_logical(b, 1) & 1]
        ta = jnp.where((a & 1) == 1, pltpu.roll(ta, 4, 0), ta)
        tb = jnp.where((b & 1) == 1, tb, pltpu.roll(tb, 4, 0))
        return jnp.where(jnp.where(low, a, b) > 3, 0.0, jnp.where(low, ta, tb))

    ng = 4 * own_ref.shape[0] // G
    attract(G, ng, True, bodies, where, ready, g_ref, *scratch)

    def finish(l, carry):
        a = acc_ref[l]
        a = a[0:4] + a[4:8]
        for q in range(3):
            g = gpos_ref[q, pl.ds(l, 1), :]
            pull_ref[q, pl.ds(l, 1), :] = (a[q : q + 1] - g * a[3:4]) * scale
        return carry

    lax.fori_loop(0, g_ref.shape[0], finish, 0, unroll=8)


def pulls(core, table, own, other, parts, gpos, scale, G=16):
    nl = gpos.shape[1]
    return pl.pallas_call(
        functools.partial(pull_kernel, G, scale, len(parts)),
        in_specs=[SMEM] * 2 + [VMEM] * 2 + [HBM] * (len(parts) + 1),
        out_shape=jax.ShapeDtypeStruct((3, nl, 128), F32),
        compiler_params=grant(51),
        scratch_shapes=[
            pltpu.VMEM((nl, 128, 128), BF16),
            pltpu.VMEM(gpos.shape, F32),
            pltpu.SemaphoreType.DMA((len(parts) + 1,)),
        ]
        + attract_scratch(nl, G),
        cost_estimate=attract_cost(8 * own.shape[0]),
    )(core, table, own, other, *parts, gpos)


def local(
    star_pos,
    star_vel,
    star_acc,
    star_jerk,
    star_mass,
    active_index,
    send_block,
    send_leaf,
    galaxy_pos,
    galaxy_mass,
):
    rows = lax.axis_size("row")
    cols = lax.axis_size("col")
    devices = rows * cols
    nb = star_pos.shape[0]
    both = ("row", "col")
    turn = lambda x: x.transpose(1, 0, 2)
    row = lax.axis_index("row").astype(I32).reshape(1)
    core = (lax.axis_index("col") & 1).astype(I32).reshape(1)
    block = send_block[0].T
    gpos = turn(galaxy_pos)
    planes, sent, start, hot = prepare(
        turn(star_pos), turn(star_vel), turn(star_acc), turn(star_jerk),
        star_mass, active_index, send_leaf[0].T, block,
    )
    arrived = lax.all_to_all(sent, both, 0, 0, tiled=True)
    stars = [planes]
    for k in range(1, rows):
        perm = [(i, (i + k) % rows) for i in range(rows)]
        stars.append(lax.ppermute(planes, "row", perm))
    g, lo = leaf_prep(gpos, galaxy_mass, 0, 1)
    leaves, table = fetch(arrived, lo)
    leaves = lax.all_to_all(leaves, both, 0, 0, tiled=True)
    parts = pair_terms(row, arrived, stars, cols)
    parts = lax.all_to_all(parts, "col", 0, 0, tiled=True)
    pos_new, mid, outgoing = correct(parts, start, planes, hot, nb, devices // 2)
    same_core = [[d for d in range(devices) if d % 2 == c] for c in range(2)]
    own = lax.all_to_all(outgoing, both, 0, 0, tiled=True, axis_index_groups=same_core)
    other = lax.ppermute(own, "col", [(i, i ^ 1) for i in range(cols)])
    vel_new = kicks(block, leaves, pos_new, mid)
    tiles = lambda x: x.reshape(-1, 2, 8, BLOCK)
    scale = STAR_DEV * devices / BLOCK
    pull = pulls(
        core, table, tiles(own), tiles(other), [g], gpos, scale
    )
    return turn(pos_new), turn(vel_new), turn(pull)


def solution(mesh):
    both = P(("row", "col"), None, None)
    flat = P(("row", "col"), None)
    return jax.shard_map(
        local,
        mesh=mesh,
        in_specs=(both, both, both, both, flat, flat, both, both, both, flat),
        out_specs=(both, both, both),
        check_vma=False,
    )
```

```python
import functools

import jax
import jax.numpy as jnp
from jax import lax
from jax.experimental import pallas as pl
from jax.experimental.pallas import tpu as pltpu
from jax.sharding import PartitionSpec as P


F32 = jnp.float32
BF16 = jnp.bfloat16
I32 = jnp.int32

STAR_DEV = 512
BLOCK = 128
STEP = 1.0
SOFT_STAR = 0.01
SOFT_GALAXY = 0.04

NT = (((1,), (1,)), ((), ()))
SMEM = pl.BlockSpec(memory_space=pltpu.SMEM)
VMEM = pl.BlockSpec(memory_space=pltpu.VMEM)
HBM = pl.BlockSpec(memory_space=pltpu.HBM)


def grant(mib):
    return pltpu.CompilerParams(vmem_limit_bytes=mib * 2**20)


def split3(x):
    a = x.astype(BF16).astype(F32)
    r = x - a
    b = r.astype(BF16).astype(F32)
    return a, b, r - b


def spread_scales(shape):
    lane = lax.broadcasted_iota(I32, shape, 1) & 63
    c = 1.0 + lane.astype(F32) * (1.0 / 128.0)
    return c, c * c * lax.rsqrt(c)


def predicted(pos, vel, acc, jerk):
    half = 0.5 * STEP**2
    sixth = STEP**3 / 6.0
    return (
        pos + STEP * vel + half * acc + sixth * jerk,
        vel + STEP * acc + half * jerk,
    )


def chosen_hot(active_row, stars):
    row = lax.broadcasted_iota(I32, (stars, active_row.shape[1]), 0)
    return jnp.where(row == active_row, 1.0, 0.0).astype(BF16)


def sum_parts(x):
    n = x.shape[0] // 3
    return x[:n] + x[n : 2 * n] + x[2 * n : 3 * n]


def pre_kernel(pos_ref, vel_ref, acc_ref, jerk_ref, mass_ref, idx_ref, leaf_ref, block_ref,
               planes_ref, sent_ref, start_ref, hot_ref):
    nb = mass_ref.shape[0]
    lanes = lambda ref, q: jnp.concatenate([ref[q, b : b + 1, :] for b in range(nb)], 1)
    rows = lambda ref: jnp.concatenate([lanes(ref, q) for q in range(3)], 0)
    flat = lambda ref: jnp.concatenate([ref[b : b + 1, :] for b in range(ref.shape[0])], 1)
    pos, vel, acc, jerk = (rows(r) for r in (pos_ref, vel_ref, acc_ref, jerk_ref))
    x, v = predicted(pos, vel, acc, jerk)
    zero1 = jnp.zeros((1, pos.shape[1]), F32)
    planes_ref[...] = jnp.concatenate([x, v, flat(mass_ref), zero1], 0)
    hot = chosen_hot(idx_ref[...], pos.shape[1])
    hot_ref[...] = hot
    zero4 = jnp.zeros((4, pos.shape[1]), F32)
    parts = split3(jnp.concatenate([pos, vel, acc, jerk, zero4], 0))
    at = sum_parts(
        jnp.dot(jnp.concatenate(parts, 0).astype(BF16), hot, preferred_element_type=F32)
    )
    start_ref[...] = at
    ax, av = predicted(at[0:3], at[3:6], at[6:9], at[9:12])
    lists = [leaf_ref[...].astype(F32), block_ref[...].astype(F32)]
    targets = sent_ref.shape[0]
    lists.append(jnp.zeros((targets - 8, targets), F32))
    lists = jnp.concatenate(lists, 0).T
    active = jnp.concatenate([ax, av], 0)
    blank = jnp.zeros((1, active.shape[1]), F32)
    for e in range(targets):
        sent_ref[e] = jnp.concatenate([active, lists[e : e + 1, :], blank], 0)


def prepare(pos, vel, acc, jerk, mass, idx, leaf, block):
    stars = mass.size
    acts = idx.shape[1]
    return pl.pallas_call(
        pre_kernel,
        out_shape=(
            jax.ShapeDtypeStruct((8, stars), F32),
            jax.ShapeDtypeStruct((block.shape[1], 8, acts), F32),
            jax.ShapeDtypeStruct((16, acts), F32),
            jax.ShapeDtypeStruct((stars, acts), BF16),
        ),
    )(pos, vel, acc, jerk, mass, idx, leaf, block)


def pair_kernel(width, row_ref, act_ref, s0_ref, s1_ref, s2_ref, s3_ref, out_ref,
                rs_ref, b_ref, ws_ref):
    own = s0_ref.shape[1]
    refs = (s0_ref, s1_ref, s2_ref, s3_ref)
    n = own * len(refs)
    acts = act_ref.shape[2]
    ic = act_ref.shape[0] * acts

    @pl.when(pl.program_id(0) == 0)
    def _():
        for k, ref in enumerate(refs):
            s = ref[...]
            row = lax.broadcasted_iota(I32, s.shape, 0)
            scale, back = spread_scales(s.shape)
            s1, s2, s3 = split3(s * scale)
            x = s[0:3]
            v = s[3:6]
            one = scale[0:1]
            n1, n2, n3 = split3(jnp.sum(x * x, 0, keepdims=True) * one)
            d1, d2, d3 = split3(jnp.sum(x * v, 0, keepdims=True) * one)
            zero7 = jnp.zeros((7, own), F32)
            tail = [one, one, one, n1, n2, n3, d1, d2, d3, zero7]
            big = jnp.concatenate([s1, s2, s3, s1, s2, s1] + tail, 0)
            rs_ref[k * own : (k + 1) * own, :] = big.T.astype(BF16)
            m = s[6:7]
            g1, g2, g3 = split3(jnp.where(row == 6, m, s * m) * back)
            b_ref[:, k * own : (k + 1) * own] = jnp.concatenate(
                [g1, g2, g3, jnp.zeros_like(g1)], 0
            ).astype(BF16)

    a = jnp.concatenate([act_ref[q] for q in range(act_ref.shape[0])], 1)
    x = a[0:3]
    v = a[3:6]
    zero2 = jnp.zeros((2, ic), F32)
    one = jnp.ones((1, ic), F32)
    zero3 = jnp.zeros((3, ic), F32)
    one3 = jnp.ones((3, ic), F32)
    zero7 = jnp.zeros((7, ic), F32)

    def left(p, extra, tail):
        p1, p2, p3 = split3(p)
        return jnp.concatenate(
            [p1, p1, p1, p2, p2, p3] + list(split3(extra)) + tail + [zero7], 0
        )

    lr = left(
        jnp.concatenate([-2.0 * x, zero3, zero2], 0),
        jnp.sum(x * x, 0, keepdims=True) + SOFT_STAR,
        [one3, zero3],
    )
    lv = left(
        jnp.concatenate([-v, -x, zero2], 0),
        jnp.sum(x * v, 0, keepdims=True),
        [zero3, one3],
    )
    L = jnp.concatenate([lr, lv], 1).astype(BF16)
    f = None
    for j0 in range(0, n, width):
        p = jnp.dot(rs_ref[j0 : j0 + width, :], L, preferred_element_type=F32)
        inv = lax.rsqrt(p[:, :ic])
        i2 = inv * inv
        w = i2 * inv
        ws_ref[j0 : j0 + width, :ic] = w.astype(BF16)
        ws_ref[j0 : j0 + width, ic:] = ((w * i2) * p[:, ic:]).astype(BF16)
        d = jnp.dot(
            b_ref[:, j0 : j0 + width],
            ws_ref[j0 : j0 + width, :],
            preferred_element_type=F32,
        )
        f = d if f is None else f + d
    t = sum_parts(f[0:24])
    wt = t[:, :ic]
    st = t[:, ic:]
    mw = wt[6:7]
    ms = st[6:7]
    acc = wt[0:3] - x * mw
    jerk = wt[3:6] - v * mw - 3.0 * (st[0:3] - x * ms)
    for q in range(act_ref.shape[0]):
        cut = slice(q * acts, (q + 1) * acts)
        out_ref[q] = jnp.concatenate([acc[:, cut], jerk[:, cut], zero2[:, cut]], 0)


def pair_terms(row, active, stars, cols, group=2, width=1024):
    acts = active.shape[2]
    own = stars[0].shape[1]
    n = own * len(stars)
    ic = group * acts
    steps = cols // group
    whole = pl.BlockSpec((8, own), lambda i, row: (0, 0))
    return pl.pallas_call(
        functools.partial(pair_kernel, width),
        grid_spec=pltpu.PrefetchScalarGridSpec(
            num_scalar_prefetch=1,
            grid=(steps,),
            in_specs=[
                pl.BlockSpec((group, 8, acts), lambda i, row: (row[0] * steps + i, 0, 0))
            ]
            + [whole] * len(stars),
            out_specs=pl.BlockSpec((group, 8, acts), lambda i, row: (i, 0, 0)),
            scratch_shapes=[
                pltpu.VMEM((n, 64), BF16),
                pltpu.VMEM((32, n), BF16),
                pltpu.VMEM((n, 2 * ic), BF16),
            ],
        ),
        out_shape=jax.ShapeDtypeStruct((cols, 8, acts), F32),
        compiler_params=grant(16),
        cost_estimate=pl.CostEstimate(
            flops=4 * 2 * 128 * cols * acts * n,
            transcendentals=cols * acts * n,
            bytes_accessed=4 * 2 * cols * 8 * acts,
        ),
    )(row, active, *stars)


def correct_kernel(part_ref, start_ref, planes_ref, hot_ref, pos_ref, mid_ref, send_ref):
    nb = pos_ref.shape[1]
    total = part_ref[0]
    for c in range(1, part_ref.shape[0]):
        total = total + part_ref[c]
    acc = total[0:3]
    jerk = total[3:6]
    x0, v0, a0, j0 = (start_ref[3 * q : 3 * q + 3, :] for q in range(4))
    v1 = v0 + (a0 + acc) * (0.5 * STEP) + (j0 - jerk) * (STEP**2 / 12.0)
    x1 = x0 + (v0 + v1) * (0.5 * STEP) + (a0 - acc) * (STEP**2 / 12.0)
    one = jnp.ones((2, x1.shape[1]), F32)
    parts = split3(jnp.concatenate([x1, v1, one], 0))
    planes = planes_ref[...]
    put = jnp.concatenate(parts + (jnp.zeros_like(parts[0]),), 0).astype(BF16)
    spread = sum_parts(
        lax.dot_general(put, hot_ref[...], NT, preferred_element_type=F32)[0:24]
    )
    new = jnp.where(spread[6:7] > 0.5, spread, planes)
    sent = []
    for b in range(nb):
        cut = slice(b * BLOCK, (b + 1) * BLOCK)
        for q in range(3):
            pos_ref[q, b : b + 1, :] = new[q : q + 1, cut]
            mid_ref[q, b : b + 1, :] = new[3 + q : 4 + q, cut]
        sent += [new[0:3, cut], planes[6:7, cut]]
    sent = jnp.concatenate(sent, 0)
    for e in range(send_ref.shape[0]):
        send_ref[e] = sent


def correct(part, start, planes, hot, nb, chips):
    return pl.pallas_call(
        correct_kernel,
        in_specs=[VMEM] * 4,
        out_shape=(
            jax.ShapeDtypeStruct((3, nb, BLOCK), F32),
            jax.ShapeDtypeStruct((3, nb, BLOCK), F32),
            jax.ShapeDtypeStruct((chips, 4 * nb, BLOCK), F32),
        ),
    )(part, start, planes, hot)


def target_terms(g):
    z1 = jnp.zeros((1, g.shape[1]), F32)
    z4 = jnp.zeros((4, g.shape[1]), F32)
    e = jnp.concatenate(split3(jnp.sum(g * g, 0, keepdims=True) + SOFT_GALAXY), 0)
    p1, p2, p3 = split3(-2.0 * g)
    low = []
    high = []
    for t in (p1, p1, p1, p2, p2, p3, jnp.ones_like(g), e):
        low += [t, z1, z4]
        high += [z4, t, z1]
    return jnp.concatenate(low + high, 0).T.astype(BF16)


def leaf_kernel(first, pos_ref, mass_ref, g_ref, lo_ref):
    z4 = jnp.zeros((4, 128), F32)

    def body(i, carry):
        l = first + i
        g = jnp.concatenate([pos_ref[q, pl.ds(l, 1), :] for q in range(3)], 0)
        g_ref[i] = target_terms(g)
        lo_ref[i] = jnp.concatenate([g, mass_ref[pl.ds(l, 1), :], z4], 0)
        return carry

    lax.fori_loop(0, g_ref.shape[0], body, 0, unroll=4)


def leaf_prep(pos, mass, part, parts):
    nl = mass.shape[0] // parts
    return pl.pallas_call(
        functools.partial(leaf_kernel, part * nl),
        out_shape=(
            jax.ShapeDtypeStruct((nl, 128, 128), BF16),
            jax.ShapeDtypeStruct((nl, 8, 128), F32),
        ),
        cost_estimate=pl.CostEstimate(
            flops=10**7, transcendentals=0, bytes_accessed=3 * 10**6
        ),
    )(pos, mass)


def gathered(parts, into, sems):
    n = parts[0].shape[0]
    return [
        pltpu.make_async_copy(p, into.at[i * n : (i + 1) * n], sems.at[i])
        for i, p in enumerate(parts)
    ]


def fetch_kernel(arrived_ref, far_ref, out_ref, table_ref, lo_ref, tab_ref, sems):
    nl = far_ref.shape[0]
    n = out_ref.shape[0]
    first = pl.program_id(0) * n

    @pl.when(pl.program_id(0) == 0)
    def _():
        leaves = pltpu.make_async_copy(far_ref, lo_ref.at[0:nl], sems.at[0])
        leaves.start()
        t = arrived_ref[:, 6, :].T[0:8, :].astype(I32)
        table_ref[...] = jnp.where(t < 0, nl, t)
        numbers = pltpu.make_async_copy(table_ref, tab_ref, sems.at[1])
        numbers.start()
        lo_ref[nl] = jnp.zeros((8, 128), F32)
        numbers.wait()
        leaves.wait()

    def body(d, carry):
        for h in range(2):
            a = lo_ref[tab_ref[2 * h, first + d]]
            b = lo_ref[tab_ref[2 * h + 1, first + d]]
            out_ref[d, 8 * h : 8 * h + 8, :] = a + pltpu.roll(b, 4, 0)
        return carry

    lax.fori_loop(0, n, body, 0, unroll=8)


def fetch(arrived, lo, steps=2):
    nl = lo.shape[0]
    devices = arrived.shape[0]
    n = devices // steps
    return pl.pallas_call(
        fetch_kernel,
        grid=(steps,),
        in_specs=[pl.BlockSpec(arrived.shape, lambda i: (0, 0, 0)), HBM],
        out_specs=(
            pl.BlockSpec((n, 16, 128), lambda i: (i, 0, 0)),
            pl.BlockSpec((8, devices), lambda i: (0, 0)),
        ),
        out_shape=(
            jax.ShapeDtypeStruct((devices, 16, 128), F32),
            jax.ShapeDtypeStruct((8, devices), I32),
        ),
        compiler_params=grant(53),
        scratch_shapes=[
            pltpu.VMEM((nl + 1, 8, 128), F32),
            pltpu.SMEM((8, devices), I32),
            pltpu.SemaphoreType.DMA((2,)),
        ],
    )(arrived, lo)


def attract(G, ng, fine, bodies, targets, ready, g_ref, acc_ref, t_ref, s_ref, v_ref):
    acc_ref[...] = jnp.zeros_like(acc_ref)
    r8 = lax.broadcasted_iota(I32, (8, 128), 0)
    low = r8 < 4
    q4 = r8 & 3
    one, back = (jnp.ones((8, 128), F32),) * 2 if fine else spread_scales((8, 128))
    zero8 = jnp.zeros((8, 128), F32)
    zero64 = jnp.zeros((64, 128), BF16)

    def prep(g, b, j):
        s = bodies(g, j, low)
        s1, s2, s3 = split3(s if fine else s * one)
        x2 = jnp.where(q4 == 3, 0.0, s * s)
        x2 = x2 + jnp.where((r8 & 1) == 0, pltpu.roll(x2, 7, 0), pltpu.roll(x2, 1, 0))
        x2 = x2 + jnp.where((r8 & 2) == 0, pltpu.roll(x2, 6, 0), pltpu.roll(x2, 2, 0))
        n1, n2, n3 = split3(x2 if fine else x2 * one)
        t1 = jnp.where(q4 == 0, n1, jnp.where(q4 == 1, n2, n3))
        m = jnp.where(
            low,
            jnp.broadcast_to(s[3:4], (8, 128)),
            jnp.broadcast_to(s[7:8], (8, 128)),
        )
        for q, t in enumerate((s1, s2, s3, t1)):
            t_ref[b, j, 8 * q : 8 * q + 8, :] = t
        weighted = jnp.where(q4 == 3, s, s * m)
        for q, t in enumerate(split3(weighted if fine else weighted * back)):
            s_ref[b, j, 8 * q : 8 * q + 8, :] = t

    def force(g, b, j):
        la, lb = targets(g, j)
        lane = lax.broadcasted_iota(I32, (128, 128), 1)
        L = jnp.where(lane < 64, g_ref[la], g_ref[lb])
        s1, s2, s3, t1 = (t_ref[b, j, 8 * q : 8 * q + 8, :] for q in range(4))
        T = jnp.concatenate([s1, s2, s3, s1, s2, s1, t1, one], 0).astype(BF16)
        W = jnp.concatenate(
            [jnp.concatenate([T, zero64], 1), jnp.concatenate([zero64, T], 1)], 0
        )
        inv = lax.rsqrt(jnp.dot(L, W, preferred_element_type=F32))
        v_ref[b, j] = inv * inv * inv

    def sums(g, b, j):
        S = jnp.concatenate([s_ref[b, j], zero8], 0).astype(BF16)
        u = v_ref[b, j]
        hi = u.astype(BF16)
        if fine:
            lo = (u - hi.astype(F32)).astype(BF16)
            S = jnp.concatenate([S, S], 1)
            V = [jnp.concatenate([t[:, :128] for t in (hi, lo)], 1)]
            V.append(jnp.concatenate([t[:, 128:] for t in (hi, lo)], 1))
        else:
            V = [hi[:, :128], hi[:, 128:]]
        f = lax.dot_general(S, jnp.concatenate(V, 0), NT, preferred_element_type=F32)
        return targets(g, j) + (sum_parts(f[0:24]),)

    def step(g, b, more, more2):
        done = []
        for j in range(G):
            done.append(sums(g, b, j))
            if more:
                force(g + 1, 1 - b, j)
            if more2:
                prep(g + 2, b, j)
        for la, lb, t in done:
            acc_ref[la] += jnp.where(low, t[:, :128], 0.0)
            acc_ref[lb] += jnp.where(low, 0.0, t[:, 128:])

    for j in range(G):
        prep(0, 0, j)
        prep(1, 1, j)
    ready()
    for j in range(G):
        force(0, 0, j)

    def body(i, carry):
        step(2 * i, 0, True, True)
        step(2 * i + 1, 1, True, True)
        return carry

    lax.fori_loop(0, ng // 2 - 1, body, 0)
    step(ng - 2, 0, True, False)
    step(ng - 1, 1, False, False)


def attract_scratch(targets, G):
    return [
        pltpu.VMEM((targets, 8, 128), F32),
        pltpu.VMEM((2, G, 32, 128), F32),
        pltpu.VMEM((2, G, 24, 128), F32),
        pltpu.VMEM((2, G, 128, 256), F32),
    ]


def attract_cost(entries):
    return pl.CostEstimate(
        flops=3 * 2 * entries * 128**3,
        transcendentals=entries * 128**2,
        bytes_accessed=entries * 4 * 512,
    )


def kick_kernel(G, block_ref, leaf_ref, pos_ref, mid_ref, vel_ref, g_ref, *scratch):
    nb = pos_ref.shape[1]
    acc_ref = scratch[0]
    place = [
        jnp.concatenate([pos_ref[q, b : b + 1, :] for q in range(3)], 0) for b in range(nb)
    ]
    for b in range(nb):
        g_ref[b] = target_terms(place[b])

    def where(g, j):
        e = g * (G // 2) + j // 2
        h = 2 * (j % 2)
        return jnp.maximum(block_ref[h, e], 0), jnp.maximum(block_ref[h + 1, e], 0)

    def bodies(g, j, low):
        h = 8 * (j % 2)
        return leaf_ref[g * (G // 2) + j // 2, h : h + 8, :]

    attract(G, 2 * leaf_ref.shape[0] // G, False, bodies, where, lambda: None, g_ref, *scratch)
    for b in range(nb):
        a = acc_ref[b]
        a = a[0:4] + a[4:8]
        kick = a[0:3] - place[b] * a[3:4]
        for q in range(3):
            vel_ref[q, b : b + 1, :] = mid_ref[q, b : b + 1, :] + STEP * kick[q : q + 1]


def kicks(block, leaves, pos, mid, G=16):
    nb = pos.shape[1]
    return pl.pallas_call(
        functools.partial(kick_kernel, G),
        in_specs=[SMEM] + [VMEM] * 3,
        out_shape=jax.ShapeDtypeStruct(mid.shape, F32),
        scratch_shapes=[pltpu.VMEM((nb, 128, 128), BF16)] + attract_scratch(nb, G),
        cost_estimate=attract_cost(4 * leaves.shape[0]),
    )(block, leaves, pos, mid)


def pull_kernel(G, scale, nparts, core_ref, tab_ref, own_ref, other_ref, *refs):
    parts = refs[:nparts]
    far_ref, pull_ref, g_ref, gpos_ref, sems = refs[nparts : nparts + 5]
    scratch = refs[nparts + 5 :]
    acc_ref = scratch[0]
    core = core_ref[0]
    copies = gathered(parts, g_ref, sems)
    copies.append(pltpu.make_async_copy(far_ref, gpos_ref, sems.at[nparts]))
    for copy in copies:
        copy.start()

    def ready():
        for copy in copies:
            copy.wait()

    def source(g, j):
        i = g * (G // 4) + j // 4
        flip = (j // 2) % 2
        return (own_ref, other_ref)[flip], i, 2 * i + (core ^ flip), 2 * (j % 2)

    def where(g, j):
        _, _, d, h = source(g, j)
        last = g_ref.shape[0] - 1
        return jnp.minimum(tab_ref[h, d], last), jnp.minimum(tab_ref[h + 1, d], last)

    def bodies(g, j, low):
        ref, i, d, h = source(g, j)
        a = tab_ref[4 + h, d]
        b = tab_ref[5 + h, d]
        ta = ref[i, lax.shift_right_logical(a, 1) & 1]
        tb = ref[i, lax.shift_right_logical(b, 1) & 1]
        ta = jnp.where((a & 1) == 1, pltpu.roll(ta, 4, 0), ta)
        tb = jnp.where((b & 1) == 1, tb, pltpu.roll(tb, 4, 0))
        return jnp.where(jnp.where(low, a, b) > 3, 0.0, jnp.where(low, ta, tb))

    ng = 4 * own_ref.shape[0] // G
    attract(G, ng, True, bodies, where, ready, g_ref, *scratch)

    weight = acc_ref[:, 3, :] + acc_ref[:, 7, :]
    for q in range(3):
        total = acc_ref[:, q, :] + acc_ref[:, 4 + q, :]
        pull_ref[q] = (total - gpos_ref[q] * weight) * scale


def pulls(core, table, own, other, parts, gpos, scale, G=32):
    nl = gpos.shape[1]
    return pl.pallas_call(
        functools.partial(pull_kernel, G, scale, len(parts)),
        in_specs=[SMEM] * 2 + [VMEM] * 2 + [HBM] * (len(parts) + 1),
        out_shape=jax.ShapeDtypeStruct((3, nl, 128), F32),
        compiler_params=grant(51),
        scratch_shapes=[
            pltpu.VMEM((nl, 128, 128), BF16),
            pltpu.VMEM(gpos.shape, F32),
            pltpu.SemaphoreType.DMA((len(parts) + 1,)),
        ]
        + attract_scratch(nl, G),
        cost_estimate=attract_cost(8 * own.shape[0]),
    )(core, table, own, other, *parts, gpos)


def local(
    star_pos,
    star_vel,
    star_acc,
    star_jerk,
    star_mass,
    active_index,
    send_block,
    send_leaf,
    galaxy_pos,
    galaxy_mass,
):
    rows = lax.axis_size("row")
    cols = lax.axis_size("col")
    devices = rows * cols
    nb = star_pos.shape[0]
    both = ("row", "col")
    turn = lambda x: x.transpose(1, 0, 2)
    row = lax.axis_index("row").astype(I32).reshape(1)
    core = (lax.axis_index("col") & 1).astype(I32).reshape(1)
    block = send_block[0].T
    gpos = turn(galaxy_pos)
    planes, sent, start, hot = prepare(
        turn(star_pos), turn(star_vel), turn(star_acc), turn(star_jerk),
        star_mass, active_index, send_leaf[0].T, block,
    )
    arrived = lax.all_to_all(sent, both, 0, 0, tiled=True)
    stars = [planes]
    for k in range(1, rows):
        perm = [(i, (i + k) % rows) for i in range(rows)]
        stars.append(lax.ppermute(planes, "row", perm))
    g, lo = leaf_prep(gpos, galaxy_mass, 0, 1)
    leaves, table = fetch(arrived, lo)
    leaves = lax.all_to_all(leaves, both, 0, 0, tiled=True)
    parts = pair_terms(row, arrived, stars, cols)
    parts = lax.all_to_all(parts, "col", 0, 0, tiled=True)
    pos_new, mid, outgoing = correct(parts, start, planes, hot, nb, devices // 2)
    same_core = [[d for d in range(devices) if d % 2 == c] for c in range(2)]
    own = lax.all_to_all(outgoing, both, 0, 0, tiled=True, axis_index_groups=same_core)
    other = lax.ppermute(own, "col", [(i, i ^ 1) for i in range(cols)])
    vel_new = kicks(block, leaves, pos_new, mid)
    tiles = lambda x: x.reshape(-1, 2, 8, BLOCK)
    scale = STAR_DEV * devices / BLOCK
    pull = pulls(
        core, table, tiles(own), tiles(other), [g], gpos, scale
    )
    return turn(pos_new), turn(vel_new), turn(pull)


def solution(mesh):
    both = P(("row", "col"), None, None)
    flat = P(("row", "col"), None)
    return jax.shard_map(
        local,
        mesh=mesh,
        in_specs=(both, both, both, both, flat, flat, both, both, both, flat),
        out_specs=(both, both, both),
        check_vma=False,
    )
```
